512 devices in a mesh: expert: 128 (over y, z, core), tensor: 4 (over x).
Axes of the slice: x: 4, y: 8, z: 8, core: 2. Of those that a mesh axis runs over, the one named last changes fastest.
Arguments:
- tokens: bfloat16 [1024, 2048], P('expert', 'tensor'), may hold values from -6 to 6
- out_grad: bfloat16 [1024, 2048], P('expert', 'tensor'), may hold values from -1.25 to 1.25
- expert_ids: int32 [1024, 8], P('expert'), may hold values from 0 to 127, all different within a row; in each aligned block of 8 rows (0 to 7, 8 to 15, ...) at most 2 rows name the same one
- gate_probs: float32 [1024, 8], P('expert'), may hold values from 0.05 to 0.45
- w_gate: bfloat16 [128, 2048, 1536], P('expert', None, 'tensor'), may hold values from -0.125 to 0.125
- w_up: bfloat16 [128, 2048, 1536], P('expert', None, 'tensor'), may hold values from -0.125 to 0.125
- w_down: bfloat16 [128, 1536, 2048], P('expert', 'tensor'), may hold values from -0.15625 to 0.15625
Outputs:
- mixed: bfloat16 [1024, 2048], P('expert', 'tensor')
- token_grad: bfloat16 [1024, 2048], P('expert', 'tensor')
- prob_grad: float32 [1024, 8], P('expert')
The draws below stay inside these ranges and needn't reach their ends.
Inputs may be any that keep to these rules, and one draw needn't show every extreme that they name: `expert_ids`: each row names 8 different experts. Within the rows of one index of expert (aligned blocks of 8 rows) no expert is named more than 2 times, a bound that some block reaches.
All inputs are finite; a program needn't handle non-finite values.
Results may differ from the reference program's by a relative error of at most 0.02.
Values may be sent and summed in bfloat16 or wider, within the bound.
No kernel may reach another device: no remote copies, remote signals or barrier semaphores. Data moves between devices by JAX's collectives and lax.ppermute only.
A program may use at most 64 MiB of HBM per device.

```python
import math
import jax
import jax.numpy as jnp
import numpy as np
from jax import lax

D = 2048
H = 1536
TOP = 8
TOK_GRP = 8
EXPERTS = 128
TOKENS = 1024
CAP = 2
N_EXPERT = 128
N_TENSOR = 4


def block_scale(stream_key, extent, shards, smallest, high):
    def one(position, parts):
        draws = jax.random.uniform(jax.random.fold_in(jax.random.fold_in(stream_key, 6), position), (parts,), jnp.float32, smallest / len(shards), high / len(shards))
        return jnp.repeat(jnp.exp(draws), extent[position] // parts).reshape((-1,) + (1,) * (len(extent) - position - 1))

    level = one(*shards[0])
    for cut in shards[1:]:
        level = level * one(*cut)
    return level


def assign_block(key, own, number, rows, amount, top, bound, lean):
    order = jax.random.permutation(key, amount)
    crowded, usual = load_shares(amount, rows * top, bound, lean, True), load_shares(amount, rows * top, bound, lean, False)
    places = jnp.arange(amount)

    def named(tallies, turn):
        used = int((tallies > 0).sum())
        fixed = max(1, used // 4)
        passed = fixed + (places - fixed + turn * (used - fixed)) % max(1, amount - fixed)
        return jnp.zeros((amount,), jnp.int32).at[order[jnp.where(places < fixed, places, passed)]].set(jnp.asarray(tallies, jnp.int32))

    tallies = jnp.where(number % 4 == 0, named(crowded, number // 4), named(usual, number - number // 4 - 1))
    mixed = jax.random.permutation(jax.random.fold_in(own, 3), amount)
    giver, receiver = mixed[0:amount // 2 * 2:2], mixed[1:amount // 2 * 2:2]
    margin = jnp.minimum(tallies[giver] - 1, bound - tallies[receiver]) // 2
    margin = jnp.where((giver == order[0]) | (receiver == order[0]) | (tallies[receiver] == 0), 0, jnp.maximum(margin, 0))
    passed = jax.random.randint(jax.random.fold_in(own, 4), (amount // 2,), 0, 1 << 20) % (margin + 1)
    tallies = tallies.at[giver].add(-passed).at[receiver].add(passed)
    items = jnp.searchsorted(jnp.cumsum(tallies), jnp.arange(rows * top), side="right").astype(jnp.int32)
    table = items.reshape(top, rows).T
    table = table[jax.random.permutation(jax.random.fold_in(own, 1), rows)]
    turn = jax.random.randint(jax.random.fold_in(own, 2), (rows, 1), 0, top)
    return jnp.take_along_axis(table, (jnp.arange(top)[None, :] + turn) % top, axis=1)


def load_shares(number_of, total, most, skew, full):
    loads = [(1 << 20) // math.isqrt(rank ** skew) + 1 for rank in range(1, number_of + 1)]
    largest = most if full else min(most, max(-(-total // number_of), total * loads[0] // sum(loads)))
    least = 1 if total - largest >= number_of - 1 else 0
    holding, surplus = [largest] + [least] * (number_of - 1), total - largest - least * (number_of - 1)
    while surplus > 0:
        movable = [i for i in range(1, number_of) if holding[i] < largest] or [i for i in range(1, number_of) if holding[i] < most]
        whole, remaining = sum([loads[i] for i in movable]), surplus
        for i in movable:
            more = min(most - holding[i], max(1, remaining * loads[i] // whole), surplus)
            holding[i] = holding[i] + more
            surplus = surplus - more
    return np.array(holding)


def scatter_about(stream_key, extent, scale, bound, cuts=(), held_as=jnp.bfloat16):
    values = scale * jax.random.normal(stream_key, extent, jnp.float32)
    if cuts:
        values = values * block_scale(stream_key, extent, cuts, -0.22, 0.18)
    return jnp.clip(values, -bound, bound).astype(held_as)


def setup_inputs(seed: int = 0) -> dict:
    key_list = jax.random.split(jax.random.key(seed), 8)
    tokens = scatter_about(key_list[0], (TOKENS, D), 1.0, 6.0, ((0, 128), (1, 4)))
    out_grad = scatter_about(key_list[1], (TOKENS, D), 0.2, 1.25, ((0, 128), (1, 4)))
    expert_ids_keys = jax.random.split(jax.random.fold_in(key_list[2], 1), TOKENS // TOK_GRP)
    expert_ids_turns = jax.random.permutation(jax.random.fold_in(key_list[2], 3), TOKENS // TOK_GRP)
    expert_ids = jax.vmap(lambda own, number: assign_block(jax.random.fold_in(key_list[2], 2), own, number, TOK_GRP, EXPERTS, TOP, CAP, 2))(expert_ids_keys, expert_ids_turns).reshape((TOKENS, TOP))
    gate_probs = jnp.clip(0.05 + 0.39999999 * jax.random.uniform(key_list[3], (TOKENS, TOP), jnp.float32) ** block_scale(key_list[3], (TOKENS, TOP), ((0, 128),), -0.2, 0.2), 0.05, 0.45)
    w_gate = scatter_about(key_list[4], (EXPERTS, D, H), D ** -0.5, 0.125, ((0, 128), (2, 4)))
    w_up = scatter_about(key_list[5], (EXPERTS, D, H), D ** -0.5, 0.125, ((0, 128), (2, 4)))
    w_down = scatter_about(key_list[6], (EXPERTS, H, D), H ** -0.5, 0.15625, ((0, 128), (1, 4)))
    return dict(tokens=tokens, out_grad=out_grad, expert_ids=expert_ids, gate_probs=gate_probs, w_gate=w_gate, w_up=w_up, w_down=w_down)


def slot_index(group_ids, expert_count, capacity):
    flat_ids = group_ids.reshape(-1).astype(jnp.int32)
    onehot = (flat_ids[:, None] == jnp.arange(expert_count, dtype=jnp.int32)[None, :]).astype(jnp.int32)
    before = jnp.cumsum(onehot, axis=0) - onehot
    slot_rank = jnp.sum(before * onehot, axis=1)
    return (flat_ids * capacity + slot_rank).astype(jnp.int32)


def expert_pass(operands):
    slot_tokens, slot_grads, gate_w, up_w, down_w = operands
    row_count = slot_tokens.shape[0]
    block_width = H // N_TENSOR
    gate_pre = jnp.dot(slot_tokens, gate_w, preferred_element_type=jnp.float32)
    up_pre = jnp.dot(slot_tokens, up_w, preferred_element_type=jnp.float32)
    gate_sig = jax.nn.sigmoid(gate_pre)
    hidden = (gate_pre * gate_sig * up_pre).astype(jnp.bfloat16)
    partials = jnp.einsum("rth,thd->trd", hidden.reshape(row_count, N_TENSOR, block_width).astype(jnp.float32),
                          down_w.reshape(N_TENSOR, block_width, D).astype(jnp.float32),
                          precision=lax.Precision.HIGHEST)
    partials = lax.optimization_barrier(partials.astype(jnp.bfloat16))
    expert_out = jnp.sum(partials.astype(jnp.float32), axis=0).astype(jnp.bfloat16)
    hidden_grad = jnp.dot(slot_grads, down_w.T, preferred_element_type=jnp.float32)
    grad_gate = (hidden_grad * up_pre * gate_sig * (1.0 + gate_pre * (1.0 - gate_sig))).astype(jnp.bfloat16)
    grad_up = (hidden_grad * gate_pre * gate_sig).astype(jnp.bfloat16)
    back_parts = jnp.einsum("rth,dth->trd", grad_gate.reshape(row_count, N_TENSOR, block_width).astype(jnp.float32),
                            gate_w.reshape(D, N_TENSOR, block_width).astype(jnp.float32),
                            precision=lax.Precision.HIGHEST)
    back_parts = back_parts + jnp.einsum("rth,dth->trd", grad_up.reshape(row_count, N_TENSOR, block_width).astype(jnp.float32),
                                         up_w.reshape(D, N_TENSOR, block_width).astype(jnp.float32),
                                         precision=lax.Precision.HIGHEST)
    back_parts = lax.optimization_barrier(back_parts.astype(jnp.bfloat16))
    expert_back = jnp.sum(back_parts.astype(jnp.float32), axis=0).astype(jnp.bfloat16)
    return expert_out, expert_back


def reference(tokens, out_grad, expert_ids, gate_probs, w_gate, w_up, w_down):
    group_count = N_EXPERT
    slot_total = EXPERTS * CAP
    slot_ids = jax.vmap(lambda group_ids: slot_index(group_ids, EXPERTS, CAP))(expert_ids.reshape(group_count, TOK_GRP, TOP))
    token_groups = tokens.reshape(group_count, TOK_GRP, D)
    grad_groups = out_grad.reshape(group_count, TOK_GRP, D)
    prob_groups = gate_probs.reshape(group_count, TOK_GRP, TOP)
    token_copies = jnp.repeat(token_groups, TOP, axis=1)
    grad_copies = (prob_groups.reshape(group_count, TOK_GRP * TOP)[:, :, None]
                   * jnp.repeat(grad_groups, TOP, axis=1).astype(jnp.float32)).astype(jnp.bfloat16)

    def place(slot_row, values):
        return jnp.zeros((slot_total, D), values.dtype).at[slot_row].set(values)

    token_slots = jax.vmap(place)(slot_ids, token_copies)
    grad_slots = jax.vmap(place)(slot_ids, grad_copies)

    def to_experts(slot_array):
        return slot_array.reshape(group_count, EXPERTS, CAP, D).transpose(1, 0, 2, 3).reshape(EXPERTS, group_count * CAP, D)

    def to_groups(expert_array):
        return expert_array.reshape(EXPERTS, group_count, CAP, D).transpose(1, 0, 2, 3).reshape(group_count, slot_total, D)

    expert_out, expert_back = lax.map(expert_pass, (to_experts(token_slots), to_experts(grad_slots), w_gate, w_up, w_down))
    out_groups = to_groups(expert_out)
    back_groups = to_groups(expert_back)
    token_out = jax.vmap(lambda table, slot_row: table[slot_row])(out_groups, slot_ids).reshape(group_count, TOK_GRP, TOP, D)
    token_back = jax.vmap(lambda table, slot_row: table[slot_row])(back_groups, slot_ids).reshape(group_count, TOK_GRP, TOP, D)
    mixed = jnp.einsum("ngk,ngkd->ngd", prob_groups, token_out.astype(jnp.float32),
                       precision=lax.Precision.HIGHEST).astype(jnp.bfloat16)
    prob_grad = jnp.einsum("ngd,ngkd->ngk", grad_groups.astype(jnp.float32), token_out.astype(jnp.float32),
                           precision=lax.Precision.HIGHEST)
    token_grad = jnp.sum(token_back.astype(jnp.float32), axis=2).astype(jnp.bfloat16)
    return (mixed.reshape(TOKENS, D), token_grad.reshape(TOKENS, D), prob_grad.reshape(TOKENS, TOP))
```

```python
import functools

import jax
import jax.numpy as jnp
from jax import lax
from jax.experimental import pallas as pl
from jax.experimental.pallas import tpu as pltpu
from jax.sharding import PartitionSpec as P

BF = jnp.bfloat16
F32 = jnp.float32


def dot(a, b, ca, cb):
    return lax.dot_general(a, b, (((ca,), (cb,)), ((), ())), preferred_element_type=F32)


def split3(v):
    hi = v.astype(BF).astype(F32)
    rest = v - hi
    mid = rest.astype(BF).astype(F32)
    return hi, mid, rest - mid


def route_maps(ids, probs, cap, slots):
    rows, top = ids.shape
    slot = lax.broadcasted_iota(jnp.int32, (rows, slots), 1)
    owner = slot // cap
    named = jnp.zeros((rows, slots), F32)
    weight = jnp.zeros((rows, slots), F32)
    for k in range(top):
        hit = ids[:, k : k + 1] == owner
        named = named + jnp.where(hit, 1.0, 0.0)
        weight = weight + jnp.where(hit, probs[:, k : k + 1], 0.0)
    before = (
        lax.broadcasted_iota(jnp.int32, (rows, rows), 0)
        > lax.broadcasted_iota(jnp.int32, (rows, rows), 1)
    ).astype(F32)
    rank = dot(before, named, 1, 0)
    fills = jnp.where(rank == (slot - owner * cap).astype(F32), named, 0.0)
    return fills, fills * weight, owner


def send_kernel(cap, ids_ref, probs_ref, tok_ref, grad_ref, tok_out, grad_out):
    fills, weighted, _ = route_maps(ids_ref[...], probs_ref[...], cap, tok_out.shape[0])
    tok_out[...] = dot(fills.astype(BF), tok_ref[...], 0, 0).astype(BF)
    parts = jnp.concatenate(split3(weighted), axis=0).astype(BF)
    grad = grad_ref[...].astype(F32)
    thrice = jnp.concatenate([grad, grad, grad], axis=0).astype(BF)
    grad_out[...] = dot(parts, thrice, 0, 0).astype(BF)


def forward_kernel(at_ref, x0, x1, x2, x3, wg, wu, wd, gate_out, up_out, o0, o1, o2, o3):
    width = x0.shape[1]
    gate = jnp.zeros(gate_out.shape, F32)
    up = jnp.zeros(gate_out.shape, F32)
    for d, x in enumerate((x0, x1, x2, x3)):
        block = lax.rem(at_ref[0] + (4 - d), 4)
        rows = pl.ds(pl.multiple_of(block * width, width), width)
        gate = gate + dot(x[...], wg[rows, :], 1, 0)
        up = up + dot(x[...], wu[rows, :], 1, 0)
    gate_out[...] = gate
    up_out[...] = up
    sig = 1.0 / (1.0 + jnp.exp(-gate))
    hidden = (gate * sig * up).astype(BF)
    for d, o in enumerate((o0, o1, o2, o3)):
        block = lax.rem(at_ref[0] + d, 4)
        cols = pl.ds(pl.multiple_of(block * width, width), width)
        o[...] = dot(hidden, wd[:, cols], 1, 0).astype(BF)


def backward_kernel(at_ref, g0, g1, g2, g3, wg, wu, wd, gate_ref, up_ref, o0, o1, o2, o3):
    width = g0.shape[1]
    hid = jnp.zeros(gate_ref.shape, F32)
    for d, g in enumerate((g0, g1, g2, g3)):
        block = lax.rem(at_ref[0] + (4 - d), 4)
        cols = pl.ds(pl.multiple_of(block * width, width), width)
        hid = hid + dot(g[...], wd[:, cols], 1, 1)
    gate = gate_ref[...]
    sig = 1.0 / (1.0 + jnp.exp(-gate))
    grad_gate = (hid * up_ref[...] * sig * (1.0 + gate * (1.0 - sig))).astype(BF)
    grad_up = (hid * gate * sig).astype(BF)
    for d, o in enumerate((o0, o1, o2, o3)):
        block = lax.rem(at_ref[0] + d, 4)
        rows = pl.ds(pl.multiple_of(block * width, width), width)
        o[...] = (dot(grad_gate, wg[rows, :], 1, 1) + dot(grad_up, wu[rows, :], 1, 1)).astype(BF)


def mix_kernel(cap, ids_ref, probs_ref, grad_ref, out_ref, mixed_ref, inner_ref):
    ids = ids_ref[...]
    rows, top = ids.shape
    got = out_ref[...]
    fills, weighted, owner = route_maps(ids, probs_ref[...], cap, got.shape[0])
    parts = jnp.concatenate(split3(weighted), axis=0).astype(BF)
    sums = dot(parts, got, 1, 0)
    mixed_ref[...] = (sums[:rows] + sums[rows : 2 * rows] + sums[2 * rows :]).astype(BF)
    inner = dot(grad_ref[...], got, 1, 1) * fills
    place = lax.broadcasted_iota(jnp.int32, (rows, top), 1)
    result = jnp.zeros((rows, top), F32)
    for k in range(top):
        one = jnp.sum(jnp.where(ids[:, k : k + 1] == owner, inner, 0.0), axis=1, keepdims=True)
        result = jnp.where(place == k, one, result)
    inner_ref[...] = result


def back_kernel(cap, ids_ref, probs_ref, back_ref, grad_out):
    got = back_ref[...]
    fills, _, _ = route_maps(ids_ref[...], probs_ref[...], cap, got.shape[0])
    grad_out[...] = dot(fills.astype(BF), got, 1, 0).astype(BF)


VM = pl.BlockSpec(memory_space=pltpu.VMEM)
SM = pl.BlockSpec(memory_space=pltpu.SMEM)
PARAMS = pltpu.CompilerParams(vmem_limit_bytes=24 << 20)


def call(kernel, args, outs, flops, scalars=0):
    specs = [SM] * scalars + [VM] * (len(args) - scalars)
    moved = sum(a.size * a.dtype.itemsize for a in args) + sum(
        o.size * o.dtype.itemsize for o in outs
    )
    return pl.pallas_call(
        kernel,
        out_shape=outs,
        in_specs=specs,
        out_specs=[VM] * len(outs),
        compiler_params=PARAMS,
        cost_estimate=pl.CostEstimate(flops=flops, bytes_accessed=moved, transcendentals=0),
    )(*args)


def shift(x, d):
    return lax.ppermute(x, "tensor", [(i, (i + d) % 4) for i in range(4)])


def per_device(tokens, out_grad, expert_ids, gate_probs, w_gate, w_up, w_down):
    experts = lax.axis_size("expert")
    rows = expert_ids.shape[0]
    width = tokens.shape[1]
    hidden = w_gate.shape[2]
    cap = 2
    slots = experts * cap
    at = lax.axis_index("tensor").astype(jnp.int32).reshape(1)
    wg, wu, wd = w_gate[0], w_up[0], w_down[0]
    table = jax.ShapeDtypeStruct((slots, width), BF)
    inner = jax.ShapeDtypeStruct((slots, hidden), F32)
    small = jax.ShapeDtypeStruct((rows, width), BF)

    def exchange(x):
        y = lax.all_to_all(
            x.reshape(experts, cap, width), "expert", split_axis=0, concat_axis=0, tiled=True
        )
        return y.reshape(slots, width)

    def gather(x):
        return x, shift(x, 1), shift(x, 2), shift(x, 3)

    def reduce(parts):
        arrived = [parts[0]] + [shift(parts[d], d) for d in (1, 2, 3)]
        return sum(a.astype(F32) for a in arrived).astype(BF)

    send_tok, send_grad = call(
        functools.partial(send_kernel, cap),
        (expert_ids, gate_probs, tokens, out_grad),
        (table, table),
        2 * slots * width * 32,
    )
    tok = gather(exchange(send_tok))
    grad = gather(exchange(send_grad))
    work = 2 * slots * width * hidden * 4
    gate_pre, up_pre, *outs = call(
        forward_kernel, (at, *tok, wg, wu, wd), (inner, inner) + (table,) * 4, 3 * work, 1
    )
    backs = call(
        backward_kernel, (at, *grad, wg, wu, wd, gate_pre, up_pre), (table,) * 4, 3 * work, 1
    )
    got_out = exchange(reduce(outs))
    got_back = exchange(reduce(backs))
    mixed, partial = call(
        functools.partial(mix_kernel, cap),
        (expert_ids, gate_probs, out_grad, got_out),
        (small, jax.ShapeDtypeStruct(expert_ids.shape, F32)),
        2 * slots * width * 32,
    )
    prob_grad = lax.psum(partial, "tensor")
    got_back, prob_grad = lax.optimization_barrier((got_back, prob_grad))
    (token_grad,) = call(
        functools.partial(back_kernel, cap),
        (expert_ids, gate_probs, got_back),
        (small,),
        2 * slots * width * 8,
    )
    return mixed, token_grad, prob_grad


def solution(mesh):
    placed = (
        P("expert", "tensor"),
        P("expert", "tensor"),
        P("expert", None),
        P("expert", None),
        P("expert", None, "tensor"),
        P("expert", None, "tensor"),
        P("expert", "tensor", None),
    )
    return jax.shard_map(
        per_device,
        mesh=mesh,
        in_specs=placed,
        out_specs=(P("expert", "tensor"), P("expert", "tensor"), P("expert", None)),
        check_vma=False,
    )
```

```python
import functools

import jax
import jax.numpy as jnp
from jax import lax
from jax.experimental import pallas as pl
from jax.experimental.pallas import tpu as pltpu
from jax.sharding import PartitionSpec as P

BF = jnp.bfloat16
F32 = jnp.float32


def dot(a, b, ca, cb):
    return lax.dot_general(a, b, (((ca,), (cb,)), ((), ())), preferred_element_type=F32)


def split2(v):
    hi = v.astype(BF).astype(F32)
    return hi, v - hi


def split3(v):
    hi, rest = split2(v)
    mid, low = split2(rest)
    return hi, mid, low


def route_maps(ids, probs, cap, slots):
    rows, top = ids.shape
    slot = lax.broadcasted_iota(jnp.int32, (rows, slots), 1)
    owner = slot // cap
    named = jnp.zeros((rows, slots), F32)
    weight = jnp.zeros((rows, slots), F32)
    for k in range(top):
        hit = ids[:, k : k + 1] == owner
        named = named + jnp.where(hit, 1.0, 0.0)
        weight = weight + jnp.where(hit, probs[:, k : k + 1], 0.0)
    before = (
        lax.broadcasted_iota(jnp.int32, (rows, rows), 0)
        > lax.broadcasted_iota(jnp.int32, (rows, rows), 1)
    ).astype(F32)
    rank = dot(before, named, 1, 0)
    fills = jnp.where(rank == (slot - owner * cap).astype(F32), named, 0.0)
    return fills, fills * weight, owner


def fetch(pairs, sems):
    copies = [pltpu.make_async_copy(s, d, sems.at[i]) for i, (s, d) in enumerate(pairs)]
    for c in copies:
        c.start()
    for c in copies:
        c.wait()


def send_kernel(cap, ids_hbm, probs_hbm, tok_hbm, grad_hbm, out, ids_ref, probs_ref, tok_ref, grad_ref, sems):
    fetch(
        ((ids_hbm, ids_ref), (probs_hbm, probs_ref), (tok_hbm, tok_ref), (grad_hbm, grad_ref)), sems
    )
    width = tok_ref.shape[1]
    fills, weighted, _ = route_maps(ids_ref[...], probs_ref[...], cap, out.shape[0])
    out[:, :width] = dot(fills.astype(BF), tok_ref[...], 0, 0).astype(BF)
    parts = jnp.concatenate(split3(weighted), axis=0).astype(BF)
    grad = grad_ref[...].astype(F32)
    thrice = jnp.concatenate([grad, grad, grad], axis=0).astype(BF)
    out[:, width:] = dot(parts, thrice, 0, 0).astype(BF)


def expert_kernel(pieces, at_ref, *refs):
    blocks = [refs[i * pieces : (i + 1) * pieces] for i in range(4)]
    stored = refs[4 * pieces : 4 * pieces + 3]
    outs = refs[4 * pieces + 3 : -4]
    wg, wu, wd, sems = refs[-4:]
    loads = [
        pltpu.make_async_copy(s, d, sems.at[i]) for i, (s, d) in enumerate(zip(stored, (wg, wu, wd)))
    ]
    for load in loads:
        load.start()
    for load in loads:
        load.wait()
    width = blocks[0][0].shape[1] // 2
    at = at_ref[0]

    def span(offset):
        return pl.ds(pl.multiple_of(lax.rem(at + (4 + offset), 4) * width, width), width)

    gate = up = hid = None
    for block, offset in zip(blocks, (0, -1, 1, 2)):
        s = span(offset)
        both = [b[...] for b in block]
        both = both[0] if pieces == 1 else jnp.concatenate(both, axis=0)
        x, g = both[:, :width], both[:, width:]
        a, b, c = dot(x, wg[s, :], 1, 0), dot(x, wu[s, :], 1, 0), dot(g, wd[:, s], 1, 1)
        gate, up, hid = (a, b, c) if gate is None else (gate + a, up + b, hid + c)
    sig = 1.0 / (1.0 + jnp.exp(-gate))
    silu = gate * sig
    hidden = (silu * up).astype(BF)
    grad_gate = (hid * up * sig * (1.0 + gate * (1.0 - sig))).astype(BF)
    grad_up = (hid * silu).astype(BF)
    inner = jnp.concatenate(split3(hid * hidden.astype(F32)), axis=1).astype(BF)
    q = dot(jnp.ones((8, inner.shape[1]), BF), inner, 1, 1)
    q_rows = q_pack(q)
    slots = hidden.shape[0]
    for i, offset in enumerate((0, 1, -1, 2)):
        s = span(offset)
        forward = dot(hidden, wd[:, s], 1, 0).astype(BF)
        back = (dot(grad_gate, wg[s, :], 1, 1) + dot(grad_up, wu[s, :], 1, 1)).astype(BF)
        if pieces == 1:
            o = outs[i]
            o[:slots, :] = forward
            o[slots : 2 * slots, :] = back
            o[2 * slots :, :] = q_rows
        else:
            outs[2 * i][...] = forward
            outs[2 * i + 1][:slots, :] = back
            outs[2 * i + 1][slots:, :] = q_rows


def q_pack(q):
    hi, low = split2(q)
    both = jnp.concatenate([hi, low], axis=1)
    return jnp.concatenate([both, both], axis=0).astype(BF)


def q_open(rows):
    both = rows.astype(F32)[:8]
    half = both.shape[1] // 2
    return both[:, :half] + both[:, half:]


def add_kernel(a, b, o):
    slots = (a.shape[0] // 256) * 256
    o[:slots, :] = (a[:slots, :].astype(F32) + b[:slots, :].astype(F32)).astype(BF)
    if slots < a.shape[0]:
        o[slots:, :] = q_pack(q_open(a[slots:, :]) + q_open(b[slots:, :]))


def join_kernel(pieces, *refs):
    o = refs[-1]
    slots = o.shape[0]
    width = refs[0].shape[1]
    if pieces == 1:
        fwd = [r[:slots, :] for r in refs[:-1]]
        bwd = [r[slots : 2 * slots, :] for r in refs[:-1]]
        qs = [r[2 * slots :, :] for r in refs[:-1]]
    else:
        half = (len(refs) - 1) // 2
        fwd = [r[...] for r in refs[:half]]
        bwd = [r[:slots, :] for r in refs[half:-1]]
        qs = [r[slots:, :] for r in refs[half:-1]]
    o[:, :width] = sum(r.astype(F32) for r in fwd).astype(BF)
    o[:, width : 2 * width] = sum(r.astype(F32) for r in bwd).astype(BF)
    hi, low = split2(sum(q_open(r) for r in qs))
    row = lax.broadcasted_iota(jnp.int32, hi.shape, 0)
    lines = jnp.where(row == 0, hi, jnp.where(row == 1, low, 0.0))
    lines = jnp.concatenate([lines, jnp.zeros((120, slots), F32)], axis=0).astype(BF)
    same = lax.broadcasted_iota(jnp.int32, (slots, slots), 0) == lax.broadcasted_iota(
        jnp.int32, (slots, slots), 1
    )
    o[:, 2 * width :] = dot(jnp.where(same, 1.0, 0.0).astype(BF), lines, 1, 1).astype(BF)


def mix_kernel(cap, ids_hbm, probs_hbm, got_ref, mixed_ref, grad_ref, prob_ref, ids_ref, probs_ref, sems):
    fetch(((ids_hbm, ids_ref), (probs_hbm, probs_ref)), sems)
    ids, probs = ids_ref[...], probs_ref[...]
    rows, top = ids.shape
    width = mixed_ref.shape[1]
    fills, weighted, owner = route_maps(ids, probs, cap, got_ref.shape[0])
    parts = jnp.concatenate(split3(weighted), axis=0).astype(BF)
    sums = dot(parts, got_ref[:, :width], 1, 0)
    mixed_ref[...] = (sums[:rows] + sums[rows : 2 * rows] + sums[2 * rows :]).astype(BF)
    grad_ref[...] = dot(fills.astype(BF), got_ref[:, width : 2 * width], 1, 0).astype(BF)
    picks = [jnp.where(ids[:, k : k + 1] == owner, fills, 0.0) for k in range(top)]
    q = dot(jnp.concatenate(picks, axis=0).astype(BF), got_ref[:, 2 * width :], 1, 0)
    q = q[:, 0:1] + q[:, 1:2]
    place = lax.broadcasted_iota(jnp.int32, (rows, top), 1)
    result = jnp.zeros((rows, top), F32)
    for k in range(top):
        result = jnp.where(place == k, q[k * rows : (k + 1) * rows], result)
    prob_ref[...] = result / probs


VM = pl.BlockSpec(memory_space=pltpu.VMEM)
SM = pl.BlockSpec(memory_space=pltpu.SMEM)
HB = pl.BlockSpec(memory_space=pltpu.MemorySpace.HBM)


def stay(x):
    return pltpu.with_memory_space_constraint(x, pltpu.MemorySpace.HBM)


def call(kernel, args, outs, flops, specs=None, scratch=(), limit=8):
    moved = sum(a.size * a.dtype.itemsize for a in (*args, *outs))
    return pl.pallas_call(
        kernel,
        out_shape=outs,
        in_specs=specs or [VM] * len(args),
        out_specs=[VM] * len(outs),
        scratch_shapes=scratch,
        compiler_params=pltpu.CompilerParams(vmem_limit_bytes=limit << 20),
        cost_estimate=pl.CostEstimate(flops=flops, bytes_accessed=moved, transcendentals=0),
    )(*args)


def shift(x, d):
    return lax.ppermute(x, "tensor", [(i, (i + d) % 4) for i in range(4)])


def like(*arrays):
    return [pltpu.VMEM(a.shape, a.dtype) for a in arrays] + [pltpu.SemaphoreType.DMA((len(arrays),))]


def per_device(tokens, out_grad, expert_ids, gate_probs, w_gate, w_up, w_down):
    experts = lax.axis_size("expert")
    width = tokens.shape[1]
    hidden = w_gate.shape[2]
    cap = 2
    slots = experts * cap
    at = lax.axis_index("tensor").astype(jnp.int32).reshape(1)

    def exchange(x):
        return lax.all_to_all(
            x.reshape(experts, cap, -1), "expert", split_axis=0, concat_axis=0, tiled=True
        )

    expert_ids, gate_probs = stay(expert_ids), stay(gate_probs)
    small = (expert_ids, gate_probs, stay(tokens), stay(out_grad))
    (send,) = call(
        functools.partial(send_kernel, cap),
        small,
        (jax.ShapeDtypeStruct((slots, 2 * width), BF),),
        2 * slots * width * 32,
        [HB] * 4,
        like(*small),
    )
    got = exchange(send)
    weights = (stay(w_gate[0]), stay(w_up[0]), stay(w_down[0]))
    work = 2 * slots * width * hidden * 24
    first = got[: experts // 2].reshape(slots // 2, 2 * width)
    second = got[experts // 2 :].reshape(slots // 2, 2 * width)
    left_first, right_second = shift(first, 1), shift(second, -1)
    left_second, right_first = shift(second, 1), shift(first, -1)
    far_first, far_second = shift(left_first, 1), shift(right_second, -1)
    blocks = (first, second, left_first, left_second, right_first, right_second, far_first, far_second)
    forward = jax.ShapeDtypeStruct((slots, width), BF)
    backward = jax.ShapeDtypeStruct((slots + 16, width), BF)
    f0, b0, f_right, b_right, f_left, b_left, f_far, b_far = call(
        functools.partial(expert_kernel, 2),
        (at, *blocks, *weights),
        (forward, backward) * 4,
        work,
        [SM] + [VM] * 8 + [HB] * 3,
        like(*weights),
        limit=24,
    )
    f_via, b_via = shift(f_far, 1), shift(b_far, -1)
    b_from_left, f_from_right = shift(b_right, 1), shift(f_left, -1)
    (f_sum,) = call(add_kernel, (f_via, f_right), (forward,), slots * width)
    (b_sum,) = call(add_kernel, (b_via, b_left), (backward,), slots * width)
    f_from_left, b_from_right = shift(f_sum, 1), shift(b_sum, -1)
    (joined,) = call(
        functools.partial(join_kernel, 2),
        (f0, f_from_left, f_from_right, b0, b_from_right, b_from_left),
        (jax.ShapeDtypeStruct((slots, 2 * width + 128), BF),),
        2 * slots * slots * 128,
    )
    back = exchange(joined)
    group = (expert_ids, gate_probs)
    return call(
        functools.partial(mix_kernel, cap),
        (*group, back.reshape(slots, -1)),
        (
            jax.ShapeDtypeStruct(tokens.shape, BF),
            jax.ShapeDtypeStruct(tokens.shape, BF),
            jax.ShapeDtypeStruct(gate_probs.shape, F32),
        ),
        2 * slots * width * 32,
        [HB] * 2 + [VM],
        like(*group),
    )


def solution(mesh):
    placed = (
        P("expert", "tensor"),
        P("expert", "tensor"),
        P("expert", None),
        P("expert", None),
        P("expert", None, "tensor"),
        P("expert", None, "tensor"),
        P("expert", "tensor", None),
    )
    return jax.shard_map(
        per_device,
        mesh=mesh,
        in_specs=placed,
        out_specs=(P("expert", "tensor"), P("expert", "tensor"), P("expert", None)),
        check_vma=False,
    )
```

```python
import functools

import jax
import jax.numpy as jnp
from jax import lax
from jax.experimental import pallas as pl
from jax.experimental.pallas import tpu as pltpu
from jax.sharding import PartitionSpec as P

BF = jnp.bfloat16
F32 = jnp.float32


def dot(a, b, ca, cb):
    return lax.dot_general(a, b, (((ca,), (cb,)), ((), ())), preferred_element_type=F32)


def split2(v):
    hi = v.astype(BF).astype(F32)
    return hi, v - hi


def split3(v):
    hi, rest = split2(v)
    mid, low = split2(rest)
    return hi, mid, low


def route_maps(ids, probs, cap, slots):
    rows, top = ids.shape
    slot = lax.broadcasted_iota(jnp.int32, (rows, slots), 1)
    owner = slot // cap
    named = jnp.zeros((rows, slots), F32)
    weight = jnp.zeros((rows, slots), F32)
    for k in range(top):
        hit = ids[:, k : k + 1] == owner
        named = named + jnp.where(hit, 1.0, 0.0)
        weight = weight + jnp.where(hit, probs[:, k : k + 1], 0.0)
    before = (
        lax.broadcasted_iota(jnp.int32, (rows, rows), 0)
        > lax.broadcasted_iota(jnp.int32, (rows, rows), 1)
    ).astype(F32)
    rank = dot(before, named, 1, 0)
    fills = jnp.where(rank == (slot - owner * cap).astype(F32), named, 0.0)
    return fills, fills * weight, owner


def fetch(pairs, sems):
    copies = [pltpu.make_async_copy(s, d, sems.at[i]) for i, (s, d) in enumerate(pairs)]
    for c in copies:
        c.start()
    for c in copies:
        c.wait()


def send_kernel(cap, ids_hbm, probs_hbm, tok_hbm, grad_hbm, out, ids_ref, probs_ref, tok_ref, grad_ref, sems):
    fetch(
        ((ids_hbm, ids_ref), (probs_hbm, probs_ref), (tok_hbm, tok_ref), (grad_hbm, grad_ref)), sems
    )
    width = tok_ref.shape[1]
    fills, weighted, _ = route_maps(ids_ref[...], probs_ref[...], cap, out.shape[0])
    out[:, :width] = dot(fills.astype(BF), tok_ref[...], 0, 0).astype(BF)
    parts = jnp.concatenate(split3(weighted), axis=0).astype(BF)
    grad = grad_ref[...].astype(F32)
    thrice = jnp.concatenate([grad, grad, grad], axis=0).astype(BF)
    out[:, width:] = dot(parts, thrice, 0, 0).astype(BF)


def expert_kernel(pieces, at_ref, *refs):
    blocks = [refs[i * pieces : (i + 1) * pieces] for i in range(4)]
    stored = refs[4 * pieces : 4 * pieces + 3]
    outs = refs[4 * pieces + 3 : -4]
    wg, wu, wd, sems = refs[-4:]
    loads = [
        pltpu.make_async_copy(s, d, sems.at[i]) for i, (s, d) in enumerate(zip(stored, (wg, wu, wd)))
    ]
    for load in loads:
        load.start()
    for load in loads:
        load.wait()
    width = blocks[0][0].shape[1] // 2
    at = at_ref[0]

    def span(offset):
        return pl.ds(pl.multiple_of(lax.rem(at + (4 + offset), 4) * width, width), width)

    gate = up = hid = None
    for block, offset in zip(blocks, (0, -1, 1, 2)):
        s = span(offset)
        both = [b[...] for b in block]
        both = both[0] if pieces == 1 else jnp.concatenate(both, axis=0)
        x, g = both[:, :width], both[:, width:]
        a, b, c = dot(x, wg[s, :], 1, 0), dot(x, wu[s, :], 1, 0), dot(g, wd[:, s], 1, 1)
        gate, up, hid = (a, b, c) if gate is None else (gate + a, up + b, hid + c)
    sig = 1.0 / (1.0 + jnp.exp(-gate))
    silu = gate * sig
    hidden = (silu * up).astype(BF)
    grad_gate = (hid * up * sig * (1.0 + gate * (1.0 - sig))).astype(BF)
    grad_up = (hid * silu).astype(BF)
    inner = jnp.concatenate(split3(hid * hidden.astype(F32)), axis=1).astype(BF)
    q = dot(jnp.ones((8, inner.shape[1]), BF), inner, 1, 1)
    q_rows = q_pack(q)
    slots = hidden.shape[0]
    for i, offset in enumerate((0, 1, -1, 2)):
        s = span(offset)
        forward = dot(hidden, wd[:, s], 1, 0).astype(BF)
        back = (dot(grad_gate, wg[s, :], 1, 1) + dot(grad_up, wu[s, :], 1, 1)).astype(BF)
        if pieces == 1:
            o = outs[i]
            o[:slots, :] = forward
            o[slots : 2 * slots, :] = back
            o[2 * slots :, :] = q_rows
        else:
            outs[2 * i][...] = forward
            outs[2 * i + 1][:slots, :] = back
            outs[2 * i + 1][slots:, :] = q_rows


def q_pack(q):
    hi, low = split2(q)
    both = jnp.concatenate([hi, low], axis=1)
    return jnp.concatenate([both, both], axis=0).astype(BF)


def q_open(rows):
    both = rows.astype(F32)[:8]
    half = both.shape[1] // 2
    return both[:, :half] + both[:, half:]


def add_kernel(a, b, o):
    slots = (a.shape[0] // 256) * 256
    o[:slots, :] = (a[:slots, :].astype(F32) + b[:slots, :].astype(F32)).astype(BF)
    if slots < a.shape[0]:
        o[slots:, :] = q_pack(q_open(a[slots:, :]) + q_open(b[slots:, :]))


def join_kernel(pieces, *refs):
    o = refs[-1]
    slots = o.shape[0]
    width = refs[0].shape[1]
    if pieces == 1:
        fwd = [r[:slots, :] for r in refs[:-1]]
        bwd = [r[slots : 2 * slots, :] for r in refs[:-1]]
        qs = [r[2 * slots :, :] for r in refs[:-1]]
    else:
        half = (len(refs) - 1) // 2
        fwd = [r[...] for r in refs[:half]]
        bwd = [r[:slots, :] for r in refs[half:-1]]
        qs = [r[slots:, :] for r in refs[half:-1]]
    o[:, :width] = sum(r.astype(F32) for r in fwd).astype(BF)
    o[:, width : 2 * width] = sum(r.astype(F32) for r in bwd).astype(BF)
    hi, low = split2(sum(q_open(r) for r in qs))
    row = lax.broadcasted_iota(jnp.int32, hi.shape, 0)
    lines = jnp.where(row == 0, hi, jnp.where(row == 1, low, 0.0))
    lines = jnp.concatenate([lines, jnp.zeros((120, slots), F32)], axis=0).astype(BF)
    same = lax.broadcasted_iota(jnp.int32, (slots, slots), 0) == lax.broadcasted_iota(
        jnp.int32, (slots, slots), 1
    )
    o[:, 2 * width :] = dot(jnp.where(same, 1.0, 0.0).astype(BF), lines, 1, 1).astype(BF)


def mix_kernel(cap, ids_hbm, probs_hbm, got_ref, mixed_ref, grad_ref, prob_ref, ids_ref, probs_ref, sems):
    fetch(((ids_hbm, ids_ref), (probs_hbm, probs_ref)), sems)
    ids, probs = ids_ref[...], probs_ref[...]
    rows, top = ids.shape
    width = mixed_ref.shape[1]
    fills, weighted, owner = route_maps(ids, probs, cap, got_ref.shape[0])
    parts = jnp.concatenate(split3(weighted), axis=0).astype(BF)
    sums = dot(parts, got_ref[:, :width], 1, 0)
    mixed_ref[...] = (sums[:rows] + sums[rows : 2 * rows] + sums[2 * rows :]).astype(BF)
    grad_ref[...] = dot(fills.astype(BF), got_ref[:, width : 2 * width], 1, 0).astype(BF)
    picks = [jnp.where(ids[:, k : k + 1] == owner, fills, 0.0) for k in range(top)]
    q = dot(jnp.concatenate(picks, axis=0).astype(BF), got_ref[:, 2 * width :], 1, 0)
    q = q[:, 0:1] + q[:, 1:2]
    place = lax.broadcasted_iota(jnp.int32, (rows, top), 1)
    result = jnp.zeros((rows, top), F32)
    for k in range(top):
        result = jnp.where(place == k, q[k * rows : (k + 1) * rows], result)
    prob_ref[...] = result / probs


VM = pl.BlockSpec(memory_space=pltpu.VMEM)
SM = pl.BlockSpec(memory_space=pltpu.SMEM)
HB = pl.BlockSpec(memory_space=pltpu.MemorySpace.HBM)


def stay(x):
    return pltpu.with_memory_space_constraint(x, pltpu.MemorySpace.HBM)


def call(kernel, args, outs, flops, specs=None, scratch=(), limit=8):
    moved = sum(a.size * a.dtype.itemsize for a in (*args, *outs))
    return pl.pallas_call(
        kernel,
        out_shape=outs,
        in_specs=specs or [VM] * len(args),
        out_specs=[VM] * len(outs),
        scratch_shapes=scratch,
        compiler_params=pltpu.CompilerParams(vmem_limit_bytes=limit << 20),
        cost_estimate=pl.CostEstimate(flops=flops, bytes_accessed=moved, transcendentals=0),
    )(*args)


def shift(x, d):
    return lax.ppermute(x, "tensor", [(i, (i + d) % 4) for i in range(4)])


def like(*arrays):
    return [pltpu.VMEM(a.shape, a.dtype) for a in arrays] + [pltpu.SemaphoreType.DMA((len(arrays),))]


def per_device(tokens, out_grad, expert_ids, gate_probs, w_gate, w_up, w_down):
    experts = lax.axis_size("expert")
    width = tokens.shape[1]
    hidden = w_gate.shape[2]
    cap = 2
    slots = experts * cap
    at = lax.axis_index("tensor").astype(jnp.int32).reshape(1)

    def exchange(x):
        return lax.all_to_all(
            x.reshape(experts, cap, -1), "expert", split_axis=0, concat_axis=0, tiled=True
        )

    expert_ids, gate_probs = stay(expert_ids), stay(gate_probs)
    small = (expert_ids, gate_probs, stay(tokens), stay(out_grad))
    (send,) = call(
        functools.partial(send_kernel, cap),
        small,
        (jax.ShapeDtypeStruct((slots, 2 * width), BF),),
        2 * slots * width * 32,
        [HB] * 4,
        like(*small),
    )
    got = exchange(send)
    weights = (stay(w_gate[0]), stay(w_up[0]), stay(w_down[0]))
    work = 2 * slots * width * hidden * 24
    own = got.reshape(slots, 2 * width)
    blocks = (own, shift(own, 1), shift(own, -1), shift(own, 2))
    piece = jax.ShapeDtypeStruct((2 * slots + 16, width), BF)
    parts = call(
        functools.partial(expert_kernel, 1),
        (at, *blocks, *weights),
        (piece,) * 4,
        work,
        [SM] + [VM] * 4 + [HB] * 3,
        like(*weights),
        limit=24,
    )
    arrived = [parts[0]] + [shift(p, d) for p, d in zip(parts[1:], (1, -1, 2))]
    (joined,) = call(
        functools.partial(join_kernel, 1),
        arrived,
        (jax.ShapeDtypeStruct((slots, 2 * width + 128), BF),),
        2 * slots * slots * 128,
    )
    back = exchange(joined)
    group = (expert_ids, gate_probs)
    return call(
        functools.partial(mix_kernel, cap),
        (*group, back.reshape(slots, -1)),
        (
            jax.ShapeDtypeStruct(tokens.shape, BF),
            jax.ShapeDtypeStruct(tokens.shape, BF),
            jax.ShapeDtypeStruct(gate_probs.shape, F32),
        ),
        2 * slots * width * 32,
        [HB] * 2 + [VM],
        like(*group),
    )


def solution(mesh):
    placed = (
        P("expert", "tensor"),
        P("expert", "tensor"),
        P("expert", None),
        P("expert", None),
        P("expert", None, "tensor"),
        P("expert", None, "tensor"),
        P("expert", "tensor", None),
    )
    return jax.shard_map(
        per_device,
        mesh=mesh,
        in_specs=placed,
        out_specs=(P("expert", "tensor"), P("expert", "tensor"), P("expert", None)),
        check_vma=False,
    )
```

```python
import functools

import jax
import jax.numpy as jnp
from jax import lax
from jax.experimental import pallas as pl
from jax.experimental.pallas import tpu as pltpu
from jax.sharding import PartitionSpec as P

BF = jnp.bfloat16
F32 = jnp.float32


def dot(a, b, ca, cb):
    return lax.dot_general(a, b, (((ca,), (cb,)), ((), ())), preferred_element_type=F32)


def split2(v):
    hi = v.astype(BF).astype(F32)
    return hi, v - hi


def split3(v):
    hi, rest = split2(v)
    mid, low = split2(rest)
    return hi, mid, low


def route_maps(ids, probs, cap, slots):
    rows, top = ids.shape
    slot = lax.broadcasted_iota(jnp.int32, (rows, slots), 1)
    owner = slot // cap
    named = jnp.zeros((rows, slots), F32)
    weight = jnp.zeros((rows, slots), F32)
    for k in range(top):
        hit = ids[:, k : k + 1] == owner
        named = named + jnp.where(hit, 1.0, 0.0)
        weight = weight + jnp.where(hit, probs[:, k : k + 1], 0.0)
    before = (
        lax.broadcasted_iota(jnp.int32, (rows, rows), 0)
        > lax.broadcasted_iota(jnp.int32, (rows, rows), 1)
    ).astype(F32)
    rank = dot(before, named, 1, 0)
    fills = jnp.where(rank == (slot - owner * cap).astype(F32), named, 0.0)
    return fills, fills * weight, owner


def fetch(pairs, sems):
    copies = [pltpu.make_async_copy(s, d, sems.at[i]) for i, (s, d) in enumerate(pairs)]
    for c in copies:
        c.start()
    for c in copies:
        c.wait()


def send_kernel(cap, ids_hbm, probs_hbm, tok_hbm, grad_hbm, out, ids_ref, probs_ref, tok_ref, grad_ref, sems):
    fetch(
        ((ids_hbm, ids_ref), (probs_hbm, probs_ref), (tok_hbm, tok_ref), (grad_hbm, grad_ref)), sems
    )
    width = tok_ref.shape[1]
    fills, weighted, _ = route_maps(ids_ref[...], probs_ref[...], cap, out.shape[0])
    out[:, :width] = dot(fills.astype(BF), tok_ref[...], 0, 0).astype(BF)
    parts = jnp.concatenate(split3(weighted), axis=0).astype(BF)
    grad = grad_ref[...].astype(F32)
    thrice = jnp.concatenate([grad, grad, grad], axis=0).astype(BF)
    out[:, width:] = dot(parts, thrice, 0, 0).astype(BF)


def span(at_ref, offset, width):
    block = lax.rem(at_ref[0] + (8 + offset * at_ref[1]), 4)
    return pl.ds(pl.multiple_of(block * width, width), width)


def products(at_ref, block, offset, wg, wu, wd):
    width = block.shape[1] // 2
    s = span(at_ref, offset, width)
    x, g = block[:, :width], block[:, width:]
    return dot(x, wg[s, :], 1, 0), dot(x, wu[s, :], 1, 0), dot(g, wd[:, s], 1, 1)


def own_kernel(at_ref, own, wg_hbm, wu_hbm, wd_hbm, gate, up, hid, wg, wu, wd, sems):
    fetch(((wg_hbm, wg), (wu_hbm, wu), (wd_hbm, wd)), sems)
    gate[...], up[...], hid[...] = products(at_ref, own, 0, wg, wu, wd)


def partial_sums(at_ref, offset, o, hidden, grad_gate, grad_up, q_rows, wg, wu, wd):
    slots, width = hidden.shape[0], o.shape[1]
    s = span(at_ref, offset, width)
    o[:slots, :] = dot(hidden, wd[:, s], 1, 0).astype(BF)
    o[slots : 2 * slots, :] = (
        dot(grad_gate, wg[s, :], 1, 1) + dot(grad_up, wu[s, :], 1, 1)
    ).astype(BF)
    o[2 * slots :, :] = q_rows


def inner_kernel(at_ref, near, other, far, gate0, up0, hid0, wg, wu, wd, o, hidden_ref, gate_ref, up_ref, q_ref):
    gate, up, hid = gate0[...], up0[...], hid0[...]
    for block, offset in ((near, -1), (other, 1), (far, 2)):
        a, b, c = products(at_ref, block, offset, wg, wu, wd)
        gate, up, hid = gate + a, up + b, hid + c
    sig = 1.0 / (1.0 + jnp.exp(-gate))
    silu = gate * sig
    hidden = (silu * up).astype(BF)
    grad_gate = (hid * up * sig * (1.0 + gate * (1.0 - sig))).astype(BF)
    grad_up = (hid * silu).astype(BF)
    inner = jnp.concatenate(split3(hid * hidden.astype(F32)), axis=1).astype(BF)
    q_rows = q_pack(dot(jnp.ones((8, inner.shape[1]), BF), inner, 1, 1))
    hidden_ref[...], gate_ref[...], up_ref[...], q_ref[...] = hidden, grad_gate, grad_up, q_rows
    partial_sums(at_ref, 2, o, hidden, grad_gate, grad_up, q_rows, wg, wu, wd)


def outer_kernel(at_ref, hidden, grad_gate, grad_up, q_ref, wg, wu, wd, near, other, own):
    for offset, o in ((-1, other), (1, near), (0, own)):
        partial_sums(
            at_ref, offset, o, hidden[...], grad_gate[...], grad_up[...], q_ref[...], wg, wu, wd
        )


def q_pack(q):
    hi, low = split2(q)
    both = jnp.concatenate([hi, low], axis=1)
    return jnp.concatenate([both, both], axis=0).astype(BF)


def q_open(rows):
    both = rows.astype(F32)[:8]
    half = both.shape[1] // 2
    return both[:, :half] + both[:, half:]


def add_kernel(a, b, o):
    rows = a.shape[0] - 16
    o[:rows, :] = (a[:rows, :].astype(F32) + b[:rows, :].astype(F32)).astype(BF)
    o[rows:, :] = q_pack(q_open(a[rows:, :]) + q_open(b[rows:, :]))


def join_kernel(*refs):
    *parts, o = refs
    slots = o.shape[0]
    width = parts[0].shape[1]
    o[:, :width] = sum(r[:slots, :].astype(F32) for r in parts).astype(BF)
    o[:, width : 2 * width] = sum(r[slots : 2 * slots, :].astype(F32) for r in parts).astype(BF)
    hi, low = split2(sum(q_open(r[2 * slots :, :]) for r in parts))
    row = lax.broadcasted_iota(jnp.int32, hi.shape, 0)
    lines = jnp.where(row == 0, hi, jnp.where(row == 1, low, 0.0))
    lines = jnp.concatenate([lines, jnp.zeros((120, slots), F32)], axis=0).astype(BF)
    same = lax.broadcasted_iota(jnp.int32, (slots, slots), 0) == lax.broadcasted_iota(
        jnp.int32, (slots, slots), 1
    )
    o[:, 2 * width :] = dot(jnp.where(same, 1.0, 0.0).astype(BF), lines, 1, 1).astype(BF)


def mix_kernel(cap, ids_ref, probs_ref, got_ref, mixed_ref, grad_ref, prob_ref):
    ids, probs = ids_ref[...], probs_ref[...]
    rows, top = ids.shape
    width = mixed_ref.shape[1]
    fills, weighted, owner = route_maps(ids, probs, cap, got_ref.shape[0])
    parts = jnp.concatenate(split3(weighted), axis=0).astype(BF)
    sums = dot(parts, got_ref[:, :width], 1, 0)
    mixed_ref[...] = (sums[:rows] + sums[rows : 2 * rows] + sums[2 * rows :]).astype(BF)
    grad_ref[...] = dot(fills.astype(BF), got_ref[:, width : 2 * width], 1, 0).astype(BF)
    picks = [jnp.where(ids[:, k : k + 1] == owner, fills, 0.0) for k in range(top)]
    q = dot(jnp.concatenate(picks, axis=0).astype(BF), got_ref[:, 2 * width :], 1, 0)
    q = q[:, 0:1] + q[:, 1:2]
    place = lax.broadcasted_iota(jnp.int32, (rows, top), 1)
    result = jnp.zeros((rows, top), F32)
    for k in range(top):
        result = jnp.where(place == k, q[k * rows : (k + 1) * rows], result)
    prob_ref[...] = result / probs


VM = pl.BlockSpec(memory_space=pltpu.VMEM)
SM = pl.BlockSpec(memory_space=pltpu.SMEM)
HB = pl.BlockSpec(memory_space=pltpu.MemorySpace.HBM)


def stay(x):
    return pltpu.with_memory_space_constraint(x, pltpu.MemorySpace.HBM)


def call(kernel, args, outs, flops, specs=None, scratch=(), limit=8):
    moved = sum(a.size * a.dtype.itemsize for a in (*args, *outs))
    return pl.pallas_call(
        kernel,
        out_shape=outs,
        in_specs=specs or [VM] * len(args),
        out_specs=[VM] * len(outs),
        scratch_shapes=list(scratch),
        compiler_params=pltpu.CompilerParams(vmem_limit_bytes=limit << 20),
        cost_estimate=pl.CostEstimate(flops=flops, bytes_accessed=moved, transcendentals=0),
    )(*args)


def shift(x, d):
    pairs = []
    for e in range(lax.axis_size("expert")):
        way = d if e % 2 == 0 else -d
        pairs += [(e * 4 + t, e * 4 + (t + way) % 4) for t in range(4)]
    return lax.ppermute(x, ("expert", "tensor"), pairs)


def like(*arrays):
    return [pltpu.VMEM(a.shape, a.dtype) for a in arrays] + [pltpu.SemaphoreType.DMA((len(arrays),))]


def per_device(tokens, out_grad, expert_ids, gate_probs, w_gate, w_up, w_down):
    experts = lax.axis_size("expert")
    width = tokens.shape[1]
    hidden = w_gate.shape[2]
    cap = 2
    slots = experts * cap
    way = 1 - 2 * (lax.axis_index("expert") % 2)
    at = jnp.stack([lax.axis_index("tensor"), way]).astype(jnp.int32)

    def exchange(x):
        return lax.all_to_all(
            x.reshape(experts, cap, -1), "expert", split_axis=0, concat_axis=0, tiled=True
        )

    expert_ids, gate_probs = stay(expert_ids), stay(gate_probs)
    small = (expert_ids, gate_probs, stay(tokens), stay(out_grad))
    send, ids, probs = call(
        functools.partial(send_kernel, cap),
        small,
        (
            jax.ShapeDtypeStruct((slots, 2 * width), BF),
            jax.ShapeDtypeStruct(expert_ids.shape, jnp.int32),
            jax.ShapeDtypeStruct(gate_probs.shape, F32),
        ),
        2 * slots * width * 32,
        [HB] * 4,
        like(*small)[2:],
    )
    got = exchange(send)
    weights = (stay(w_gate[0]), stay(w_up[0]), stay(w_down[0]))
    work = 2 * slots * width * hidden * 24
    own = got.reshape(slots, 2 * width)
    near = shift(own, 1)
    other = shift(own, -1)
    far = shift(near, 1)
    acc = jax.ShapeDtypeStruct((slots, hidden), F32)
    act = jax.ShapeDtypeStruct((slots, hidden), BF)
    piece = jax.ShapeDtypeStruct((2 * slots + 16, width), BF)
    held = [jax.ShapeDtypeStruct(w.shape, w.dtype) for w in weights]
    *first, wg, wu, wd = call(
        own_kernel,
        (at, own, *weights),
        (acc,) * 3 + tuple(held),
        work // 8,
        [SM, VM] + [HB] * 3,
        [pltpu.SemaphoreType.DMA((3,))],
    )
    part_far, *kept = call(
        inner_kernel,
        (at, near, other, far, *first, wg, wu, wd),
        (piece, act, act, act, jax.ShapeDtypeStruct((16, width), BF)),
        work // 2,
        [SM] + [VM] * 9,
        limit=16,
    )
    via = shift(part_far, 1)
    part_near, part_other, part_own = call(
        outer_kernel, (at, *kept, wg, wu, wd), (piece,) * 3, 3 * work // 8, [SM] + [VM] * 7, limit=16
    )
    from_other = shift(part_other, -1)
    (summed,) = call(add_kernel, (via, part_near), (piece,), slots * width)
    from_near = shift(summed, 1)
    (joined,) = call(
        join_kernel,
        (part_own, from_other, from_near),
        (jax.ShapeDtypeStruct((slots, 2 * width + 128), BF),),
        2 * slots * slots * 128,
    )
    back = exchange(joined)
    return call(
        functools.partial(mix_kernel, cap),
        (ids, probs, back.reshape(slots, -1)),
        (
            jax.ShapeDtypeStruct(tokens.shape, BF),
            jax.ShapeDtypeStruct(tokens.shape, BF),
            jax.ShapeDtypeStruct(gate_probs.shape, F32),
        ),
        2 * slots * width * 32,
    )


def solution(mesh):
    placed = (
        P("expert", "tensor"),
        P("expert", "tensor"),
        P("expert", None),
        P("expert", None),
        P("expert", None, "tensor"),
        P("expert", None, "tensor"),
        P("expert", "tensor", None),
    )
    return jax.shard_map(
        per_device,
        mesh=mesh,
        in_specs=placed,
        out_specs=(P("expert", "tensor"), P("expert", "tensor"), P("expert", None)),
        check_vma=False,
    )
```

```python
import functools

import jax
import jax.numpy as jnp
from jax import lax
from jax.experimental import pallas as pl
from jax.experimental.pallas import tpu as pltpu
from jax.sharding import PartitionSpec as P

BF = jnp.bfloat16
F32 = jnp.float32


def dot(a, b, ca, cb):
    return lax.dot_general(a, b, (((ca,), (cb,)), ((), ())), preferred_element_type=F32)


def split2(v):
    hi = v.astype(BF).astype(F32)
    return hi, v - hi


def split3(v):
    hi, rest = split2(v)
    mid, low = split2(rest)
    return hi, mid, low


def route_maps(ids, probs, cap, slots):
    rows, top = ids.shape
    slot = lax.broadcasted_iota(jnp.int32, (rows, slots), 1)
    owner = slot // cap
    named = jnp.zeros((rows, slots), F32)
    weight = jnp.zeros((rows, slots), F32)
    for k in range(top):
        hit = ids[:, k : k + 1] == owner
        named = named + jnp.where(hit, 1.0, 0.0)
        weight = weight + jnp.where(hit, probs[:, k : k + 1], 0.0)
    before = (
        lax.broadcasted_iota(jnp.int32, (rows, rows), 0)
        > lax.broadcasted_iota(jnp.int32, (rows, rows), 1)
    ).astype(F32)
    rank = dot(before, named, 1, 0)
    fills = jnp.where(rank == (slot - owner * cap).astype(F32), named, 0.0)
    return fills, fills * weight, owner


def fetch(pairs, sems):
    copies = [pltpu.make_async_copy(s, d, sems.at[i]) for i, (s, d) in enumerate(pairs)]
    for c in copies:
        c.start()
    for c in copies:
        c.wait()


def send_kernel(cap, ids_hbm, probs_hbm, tok_hbm, grad_hbm, out, ids_ref, probs_ref, tok_ref, grad_ref, sems):
    fetch(
        ((ids_hbm, ids_ref), (probs_hbm, probs_ref), (tok_hbm, tok_ref), (grad_hbm, grad_ref)), sems
    )
    width = tok_ref.shape[1]
    fills, weighted, _ = route_maps(ids_ref[...], probs_ref[...], cap, out.shape[0])
    out[:, :width] = dot(fills.astype(BF), tok_ref[...], 0, 0).astype(BF)
    parts = jnp.concatenate(split3(weighted), axis=0).astype(BF)
    grad = grad_ref[...].astype(F32)
    thrice = jnp.concatenate([grad, grad, grad], axis=0).astype(BF)
    out[:, width:] = dot(parts, thrice, 0, 0).astype(BF)


def span(at_ref, offset, width):
    block = lax.rem(at_ref[0] + (4 + offset), 4)
    return pl.ds(pl.multiple_of(block * width, width), width)


def forward_kernel(at_ref, own, left, right, far, wg_hbm, wu_hbm, wd_hbm, *refs):
    *outs, slope_ref, silu_ref, hidden_ref, wg, wu, wd, sems = refs
    loads = [
        pltpu.make_async_copy(s, d, sems.at[i])
        for i, (s, d) in enumerate(((wg_hbm, wg), (wu_hbm, wu), (wd_hbm, wd)))
    ]
    for load in loads:
        load.start()
    loads[0].wait()
    loads[1].wait()
    width = own.shape[1]
    gate = up = 0.0
    for block, offset in ((own, 0), (left, -1), (right, 1), (far, 2)):
        s = span(at_ref, offset, width)
        gate = gate + dot(block[...], wg[s, :], 1, 0)
        up = up + dot(block[...], wu[s, :], 1, 0)
    sig = 1.0 / (1.0 + jnp.exp(-gate))
    silu = gate * sig
    hidden = (silu * up).astype(BF)
    slope_ref[...] = up * sig * (1.0 + gate * (1.0 - sig))
    silu_ref[...] = silu
    hidden_ref[...] = hidden
    loads[2].wait()
    for offset, o in zip((2, -1, 1, 0), outs):
        o[...] = dot(hidden, wd[:, span(at_ref, offset, width)], 1, 0).astype(BF)


def backward_kernel(at_ref, own, left, right, far, slope, silu, hidden, wg, wu, wd, *outs):
    width = own.shape[1]
    hid = 0.0
    for block, offset in ((own, 0), (left, -1), (right, 1), (far, 2)):
        hid = hid + dot(block[...], wd[:, span(at_ref, offset, width)], 1, 1)
    grad_gate = (hid * slope[...]).astype(BF)
    grad_up = (hid * silu[...]).astype(BF)
    inner = jnp.concatenate(split3(hid * hidden[...].astype(F32)), axis=1).astype(BF)
    q_rows = q_pack(dot(jnp.ones((8, inner.shape[1]), BF), inner, 1, 1))
    slots = hidden.shape[0]
    for offset, o in zip((2, -1, 1, 0), outs):
        s = span(at_ref, offset, width)
        o[:slots, :] = (dot(grad_gate, wg[s, :], 1, 1) + dot(grad_up, wu[s, :], 1, 1)).astype(BF)
        o[slots:, :] = q_rows


def q_pack(q):
    hi, low = split2(q)
    both = jnp.concatenate([hi, low], axis=1)
    return jnp.concatenate([both, both], axis=0).astype(BF)


def q_open(rows):
    both = rows.astype(F32)[:8]
    half = both.shape[1] // 2
    return both[:, :half] + both[:, half:]


def add_kernel(a, b, o):
    slots = a.shape[0] // 256 * 256
    o[:slots, :] = (a[:slots, :].astype(F32) + b[:slots, :].astype(F32)).astype(BF)
    if slots < a.shape[0]:
        o[slots:, :] = q_pack(q_open(a[slots:, :]) + q_open(b[slots:, :]))


def join_kernel(*refs):
    fwd, bwd, o = refs[:3], refs[3:6], refs[6]
    slots = o.shape[0]
    width = fwd[0].shape[1]
    o[:, :width] = sum(r[...].astype(F32) for r in fwd).astype(BF)
    o[:, width : 2 * width] = sum(r[:slots, :].astype(F32) for r in bwd).astype(BF)
    hi, low = split2(sum(q_open(r[slots:, :]) for r in bwd))
    row = lax.broadcasted_iota(jnp.int32, hi.shape, 0)
    lines = jnp.where(row == 0, hi, jnp.where(row == 1, low, 0.0))
    lines = jnp.concatenate([lines, jnp.zeros((120, slots), F32)], axis=0).astype(BF)
    same = lax.broadcasted_iota(jnp.int32, (slots, slots), 0) == lax.broadcasted_iota(
        jnp.int32, (slots, slots), 1
    )
    o[:, 2 * width :] = dot(jnp.where(same, 1.0, 0.0).astype(BF), lines, 1, 1).astype(BF)


def mix_kernel(cap, ids_ref, probs_ref, got_ref, mixed_ref, grad_ref, prob_ref):
    ids, probs = ids_ref[...], probs_ref[...]
    rows, top = ids.shape
    width = mixed_ref.shape[1]
    fills, weighted, owner = route_maps(ids, probs, cap, got_ref.shape[0])
    parts = jnp.concatenate(split3(weighted), axis=0).astype(BF)
    sums = dot(parts, got_ref[:, :width], 1, 0)
    mixed_ref[...] = (sums[:rows] + sums[rows : 2 * rows] + sums[2 * rows :]).astype(BF)
    grad_ref[...] = dot(fills.astype(BF), got_ref[:, width : 2 * width], 1, 0).astype(BF)
    picks = [jnp.where(ids[:, k : k + 1] == owner, fills, 0.0) for k in range(top)]
    q = dot(jnp.concatenate(picks, axis=0).astype(BF), got_ref[:, 2 * width :], 1, 0)
    q = q[:, 0:1] + q[:, 1:2]
    place = lax.broadcasted_iota(jnp.int32, (rows, top), 1)
    result = jnp.zeros((rows, top), F32)
    for k in range(top):
        result = jnp.where(place == k, q[k * rows : (k + 1) * rows], result)
    prob_ref[...] = result / probs


VM = pl.BlockSpec(memory_space=pltpu.VMEM)
SM = pl.BlockSpec(memory_space=pltpu.SMEM)
HB = pl.BlockSpec(memory_space=pltpu.MemorySpace.HBM)


def stay(x):
    return pltpu.with_memory_space_constraint(x, pltpu.MemorySpace.HBM)


def call(kernel, args, outs, flops, specs=None, scratch=(), limit=8):
    moved = sum(a.size * a.dtype.itemsize for a in (*args, *outs))
    return pl.pallas_call(
        kernel,
        out_shape=outs,
        in_specs=specs or [VM] * len(args),
        out_specs=[VM] * len(outs),
        scratch_shapes=list(scratch),
        compiler_params=pltpu.CompilerParams(vmem_limit_bytes=limit << 20),
        cost_estimate=pl.CostEstimate(flops=flops, bytes_accessed=moved, transcendentals=0),
    )(*args)


def shift(x, d):
    return lax.ppermute(x, "tensor", [(i, (i + d) % 4) for i in range(4)])


def like(*arrays):
    return [pltpu.VMEM(a.shape, a.dtype) for a in arrays] + [pltpu.SemaphoreType.DMA((len(arrays),))]


def per_device(tokens, out_grad, expert_ids, gate_probs, w_gate, w_up, w_down):
    experts = lax.axis_size("expert")
    width = tokens.shape[1]
    hidden = w_gate.shape[2]
    cap = 2
    slots = experts * cap
    at = lax.axis_index("tensor").astype(jnp.int32).reshape(1)

    def exchange(x):
        return lax.all_to_all(
            x.reshape(experts, cap, -1), "expert", split_axis=0, concat_axis=0, tiled=True
        )

    expert_ids, gate_probs = stay(expert_ids), stay(gate_probs)
    small = (expert_ids, gate_probs, stay(tokens), stay(out_grad))
    send, ids, probs = call(
        functools.partial(send_kernel, cap),
        small,
        (
            jax.ShapeDtypeStruct((slots, 2 * width), BF),
            jax.ShapeDtypeStruct(expert_ids.shape, jnp.int32),
            jax.ShapeDtypeStruct(gate_probs.shape, F32),
        ),
        2 * slots * width * 32,
        [HB] * 4,
        like(*small)[2:],
    )
    got = exchange(send)
    weights = (stay(w_gate[0]), stay(w_up[0]), stay(w_down[0]))
    work = 2 * slots * width * hidden * 24
    tok = got[:, :, :width].reshape(slots, width)
    grad = got[:, :, width:].reshape(slots, width)
    tok_left, tok_right = shift(tok, 1), shift(tok, -1)
    tok_far = shift(tok_left, 1)
    grad_right, grad_left = shift(grad, -1), shift(grad, 1)
    grad_far = shift(grad_right, -1)
    tok_far, grad_left = lax.optimization_barrier((tok_far, grad_left))
    acc = jax.ShapeDtypeStruct((slots, hidden), F32)
    act = jax.ShapeDtypeStruct((slots, hidden), BF)
    table = jax.ShapeDtypeStruct((slots, width), BF)
    longer = jax.ShapeDtypeStruct((slots + 16, width), BF)
    held = [jax.ShapeDtypeStruct(w.shape, w.dtype) for w in weights]
    out_far, out_left, out_right, out_own, *kept = call(
        forward_kernel,
        (at, tok, tok_left, tok_right, tok_far, *weights),
        (table,) * 4 + (acc, acc, act) + tuple(held),
        1,
        [SM] + [VM] * 4 + [HB] * 3,
        [pltpu.SemaphoreType.DMA((3,))],
        limit=20,
    )
    out_via, out_from_right = shift(out_far, 1), shift(out_left, -1)
    (out_sum,) = call(add_kernel, (out_via, out_right), (table,), slots * width)
    out_sum, out_from_right, grad_far = lax.optimization_barrier((out_sum, out_from_right, grad_far))
    out_from_left = shift(out_sum, 1)
    back_far, back_left, back_right, back_own = call(
        backward_kernel,
        (at, grad, grad_left, grad_right, grad_far, *kept),
        (longer,) * 4,
        1,
        [SM] + [VM] * 10,
        limit=20,
    )
    back_via, back_from_left = shift(back_far, -1), shift(back_right, 1)
    (back_sum,) = call(add_kernel, (back_via, back_left), (longer,), slots * width)
    back_from_right = shift(back_sum, -1)
    (joined,) = call(
        join_kernel,
        (out_own, out_from_left, out_from_right, back_own, back_from_left, back_from_right),
        (jax.ShapeDtypeStruct((slots, 2 * width + 128), BF),),
        2 * slots * slots * 128,
    )
    back = exchange(joined)
    return call(
        functools.partial(mix_kernel, cap),
        (ids, probs, back.reshape(slots, -1)),
        (
            jax.ShapeDtypeStruct(tokens.shape, BF),
            jax.ShapeDtypeStruct(tokens.shape, BF),
            jax.ShapeDtypeStruct(gate_probs.shape, F32),
        ),
        2 * slots * width * 32,
    )


def solution(mesh):
    placed = (
        P("expert", "tensor"),
        P("expert", "tensor"),
        P("expert", None),
        P("expert", None),
        P("expert", None, "tensor"),
        P("expert", None, "tensor"),
        P("expert", "tensor", None),
    )
    return jax.shard_map(
        per_device,
        mesh=mesh,
        in_specs=placed,
        out_specs=(P("expert", "tensor"), P("expert", "tensor"), P("expert", None)),
        check_vma=False,
    )
```

```python
import functools

import jax
import jax.numpy as jnp
from jax import lax
from jax.experimental import pallas as pl
from jax.experimental.pallas import tpu as pltpu
from jax.sharding import PartitionSpec as P

BF = jnp.bfloat16
F32 = jnp.float32


def dot(a, b, ca, cb):
    return lax.dot_general(a, b, (((ca,), (cb,)), ((), ())), preferred_element_type=F32)


def split2(v):
    hi = v.astype(BF).astype(F32)
    return hi, v - hi


def split3(v):
    hi, rest = split2(v)
    mid, low = split2(rest)
    return hi, mid, low


def route_maps(ids, probs, cap, slots):
    rows, top = ids.shape
    slot = lax.broadcasted_iota(jnp.int32, (rows, slots), 1)
    owner = slot // cap
    named = jnp.zeros((rows, slots), F32)
    weight = jnp.zeros((rows, slots), F32)
    for k in range(top):
        hit = ids[:, k : k + 1] == owner
        named = named + jnp.where(hit, 1.0, 0.0)
        weight = weight + jnp.where(hit, probs[:, k : k + 1], 0.0)
    before = (
        lax.broadcasted_iota(jnp.int32, (rows, rows), 0)
        > lax.broadcasted_iota(jnp.int32, (rows, rows), 1)
    ).astype(F32)
    rank = dot(before, named, 1, 0)
    fills = jnp.where(rank == (slot - owner * cap).astype(F32), named, 0.0)
    return fills, fills * weight, owner


def fetch(pairs, sems):
    copies = [pltpu.make_async_copy(s, d, sems.at[i]) for i, (s, d) in enumerate(pairs)]
    for c in copies:
        c.start()
    for c in copies:
        c.wait()


def send_kernel(cap, ids_hbm, probs_hbm, tok_hbm, grad_hbm, out, ids_ref, probs_ref, tok_ref, grad_ref, sems):
    fetch(
        ((ids_hbm, ids_ref), (probs_hbm, probs_ref), (tok_hbm, tok_ref), (grad_hbm, grad_ref)), sems
    )
    width = tok_ref.shape[1]
    fills, weighted, _ = route_maps(ids_ref[...], probs_ref[...], cap, out.shape[0])
    out[:, :width] = dot(fills.astype(BF), tok_ref[...], 0, 0).astype(BF)
    parts = jnp.concatenate(split3(weighted), axis=0).astype(BF)
    grad = grad_ref[...].astype(F32)
    thrice = jnp.concatenate([grad, grad, grad], axis=0).astype(BF)
    out[:, width:] = dot(parts, thrice, 0, 0).astype(BF)


def span(at_ref, offset, width):
    block = lax.rem(at_ref[0] + (4 + offset), 4)
    return pl.ds(pl.multiple_of(block * width, width), width)


def products(at_ref, halves, offset, wg, wu, wd):
    both = jnp.concatenate([h[...] for h in halves], axis=0)
    width = both.shape[1] // 2
    s = span(at_ref, offset, width)
    x, g = both[:, :width], both[:, width:]
    return dot(x, wg[s, :], 1, 0), dot(x, wu[s, :], 1, 0), dot(g, wd[:, s], 1, 1)


def early_kernel(at_ref, o1, o2, l1, l2, r1, r2, wg_hbm, wu_hbm, wd_hbm, gate, up, hid, wg, wu, wd, sems):
    fetch(((wg_hbm, wg), (wu_hbm, wu), (wd_hbm, wd)), sems)
    totals = products(at_ref, (o1, o2), 0, wg, wu, wd)
    for halves, offset in (((l1, l2), -1), ((r1, r2), 1)):
        totals = [t + p for t, p in zip(totals, products(at_ref, halves, offset, wg, wu, wd))]
    gate[...], up[...], hid[...] = totals


def late_kernel(at_ref, f1, f2, gate0, up0, hid0, wg, wu, wd, *outs):
    gate, up, hid = [
        t[...] + p for t, p in zip((gate0, up0, hid0), products(at_ref, (f1, f2), 2, wg, wu, wd))
    ]
    sig = 1.0 / (1.0 + jnp.exp(-gate))
    silu = gate * sig
    hidden = (silu * up).astype(BF)
    grad_gate = (hid * up * sig * (1.0 + gate * (1.0 - sig))).astype(BF)
    grad_up = (hid * silu).astype(BF)
    inner = jnp.concatenate(split3(hid * hidden.astype(F32)), axis=1).astype(BF)
    q_rows = q_pack(dot(jnp.ones((8, inner.shape[1]), BF), inner, 1, 1))
    slots, width = outs[0].shape
    for i, offset in enumerate((2, 1, -1, 0)):
        s = span(at_ref, offset, width)
        outs[2 * i][...] = dot(hidden, wd[:, s], 1, 0).astype(BF)
        o = outs[2 * i + 1]
        o[:slots, :] = (dot(grad_gate, wg[s, :], 1, 1) + dot(grad_up, wu[s, :], 1, 1)).astype(BF)
        o[slots:, :] = q_rows


def q_pack(q):
    hi, low = split2(q)
    both = jnp.concatenate([hi, low], axis=1)
    return jnp.concatenate([both, both], axis=0).astype(BF)


def q_open(rows):
    both = rows.astype(F32)[:8]
    half = both.shape[1] // 2
    return both[:, :half] + both[:, half:]


def add_kernel(a, b, o):
    slots = a.shape[0] // 256 * 256
    o[:slots, :] = (a[:slots, :].astype(F32) + b[:slots, :].astype(F32)).astype(BF)
    if slots < a.shape[0]:
        o[slots:, :] = q_pack(q_open(a[slots:, :]) + q_open(b[slots:, :]))


def join_kernel(*refs):
    fwd, bwd, o = refs[:3], refs[3:6], refs[6]
    slots = o.shape[0]
    width = fwd[0].shape[1]
    o[:, :width] = sum(r[...].astype(F32) for r in fwd).astype(BF)
    o[:, width : 2 * width] = sum(r[:slots, :].astype(F32) for r in bwd).astype(BF)
    hi, low = split2(sum(q_open(r[slots:, :]) for r in bwd))
    row = lax.broadcasted_iota(jnp.int32, hi.shape, 0)
    lines = jnp.where(row == 0, hi, jnp.where(row == 1, low, 0.0))
    lines = jnp.concatenate([lines, jnp.zeros((120, slots), F32)], axis=0).astype(BF)
    same = lax.broadcasted_iota(jnp.int32, (slots, slots), 0) == lax.broadcasted_iota(
        jnp.int32, (slots, slots), 1
    )
    o[:, 2 * width :] = dot(jnp.where(same, 1.0, 0.0).astype(BF), lines, 1, 1).astype(BF)


def mix_kernel(cap, ids_ref, probs_ref, got_ref, mixed_ref, grad_ref, prob_ref):
    ids, probs = ids_ref[...], probs_ref[...]
    rows, top = ids.shape
    width = mixed_ref.shape[1]
    fills, weighted, owner = route_maps(ids, probs, cap, got_ref.shape[0])
    parts = jnp.concatenate(split3(weighted), axis=0).astype(BF)
    sums = dot(parts, got_ref[:, :width], 1, 0)
    mixed_ref[...] = (sums[:rows] + sums[rows : 2 * rows] + sums[2 * rows :]).astype(BF)
    grad_ref[...] = dot(fills.astype(BF), got_ref[:, width : 2 * width], 1, 0).astype(BF)
    picks = [jnp.where(ids[:, k : k + 1] == owner, fills, 0.0) for k in range(top)]
    q = dot(jnp.concatenate(picks, axis=0).astype(BF), got_ref[:, 2 * width :], 1, 0)
    q = q[:, 0:1] + q[:, 1:2]
    place = lax.broadcasted_iota(jnp.int32, (rows, top), 1)
    result = jnp.zeros((rows, top), F32)
    for k in range(top):
        result = jnp.where(place == k, q[k * rows : (k + 1) * rows], result)
    prob_ref[...] = result / probs


VM = pl.BlockSpec(memory_space=pltpu.VMEM)
SM = pl.BlockSpec(memory_space=pltpu.SMEM)
HB = pl.BlockSpec(memory_space=pltpu.MemorySpace.HBM)


def stay(x):
    return pltpu.with_memory_space_constraint(x, pltpu.MemorySpace.HBM)


def call(kernel, args, outs, flops, specs=None, scratch=(), limit=8):
    moved = sum(a.size * a.dtype.itemsize for a in (*args, *outs))
    return pl.pallas_call(
        kernel,
        out_shape=outs,
        in_specs=specs or [VM] * len(args),
        out_specs=[VM] * len(outs),
        scratch_shapes=list(scratch),
        compiler_params=pltpu.CompilerParams(vmem_limit_bytes=limit << 20),
        cost_estimate=pl.CostEstimate(flops=flops, bytes_accessed=moved, transcendentals=0),
    )(*args)


def shift(x, d):
    return lax.ppermute(x, "tensor", [(i, (i + d) % 4) for i in range(4)])


def like(*arrays):
    return [pltpu.VMEM(a.shape, a.dtype) for a in arrays] + [pltpu.SemaphoreType.DMA((len(arrays),))]


def per_device(tokens, out_grad, expert_ids, gate_probs, w_gate, w_up, w_down):
    experts = lax.axis_size("expert")
    width = tokens.shape[1]
    hidden = w_gate.shape[2]
    cap = 2
    slots = experts * cap
    at = lax.axis_index("tensor").astype(jnp.int32).reshape(1)

    def exchange(x):
        return lax.all_to_all(
            x.reshape(experts, cap, -1), "expert", split_axis=0, concat_axis=0, tiled=True
        )

    expert_ids, gate_probs = stay(expert_ids), stay(gate_probs)
    small = (expert_ids, gate_probs, stay(tokens), stay(out_grad))
    send, ids, probs = call(
        functools.partial(send_kernel, cap),
        small,
        (
            jax.ShapeDtypeStruct((slots, 2 * width), BF),
            jax.ShapeDtypeStruct(expert_ids.shape, jnp.int32),
            jax.ShapeDtypeStruct(gate_probs.shape, F32),
        ),
        2 * slots * width * 32,
        [HB] * 4,
        like(*small)[2:],
    )
    got = exchange(send)
    weights = (stay(w_gate[0]), stay(w_up[0]), stay(w_down[0]))
    work = 2 * slots * width * hidden * 24
    first = got[: experts // 2].reshape(slots // 2, 2 * width)
    second = got[experts // 2 :].reshape(slots // 2, 2 * width)
    left_first, right_second = shift(first, 1), shift(second, -1)
    left_second, right_first = shift(second, 1), shift(first, -1)
    far_first, far_second = shift(left_first, 1), shift(right_second, -1)
    acc = jax.ShapeDtypeStruct((slots, hidden), F32)
    table = jax.ShapeDtypeStruct((slots, width), BF)
    longer = jax.ShapeDtypeStruct((slots + 16, width), BF)
    held = [jax.ShapeDtypeStruct(w.shape, w.dtype) for w in weights]
    known = call(
        early_kernel,
        (at, first, second, left_first, left_second, right_first, right_second, *weights),
        (acc,) * 3 + tuple(held),
        3 * work // 8,
        [SM] + [VM] * 6 + [HB] * 3,
        [pltpu.SemaphoreType.DMA((3,))],
        limit=20,
    )
    out_far, back_far, out_right, back_right, out_left, back_left, out_own, back_own = call(
        late_kernel,
        (at, far_first, far_second, *known),
        (table, longer) * 4,
        5 * work // 8,
        [SM] + [VM] * 8,
        limit=20,
    )
    out_via, back_via = shift(out_far, 1), shift(back_far, -1)
    back_from_left, out_from_right = shift(back_right, 1), shift(out_left, -1)
    (out_sum,) = call(add_kernel, (out_via, out_right), (table,), slots * width)
    (back_sum,) = call(add_kernel, (back_via, back_left), (longer,), slots * width)
    out_from_left, back_from_right = shift(out_sum, 1), shift(back_sum, -1)
    (joined,) = call(
        join_kernel,
        (out_own, out_from_left, out_from_right, back_own, back_from_left, back_from_right),
        (jax.ShapeDtypeStruct((slots, 2 * width + 128), BF),),
        2 * slots * slots * 128,
    )
    back = exchange(joined)
    return call(
        functools.partial(mix_kernel, cap),
        (ids, probs, back.reshape(slots, -1)),
        (
            jax.ShapeDtypeStruct(tokens.shape, BF),
            jax.ShapeDtypeStruct(tokens.shape, BF),
            jax.ShapeDtypeStruct(gate_probs.shape, F32),
        ),
        2 * slots * width * 32,
    )


def solution(mesh):
    placed = (
        P("expert", "tensor"),
        P("expert", "tensor"),
        P("expert", None),
        P("expert", None),
        P("expert", None, "tensor"),
        P("expert", None, "tensor"),
        P("expert", "tensor", None),
    )
    return jax.shard_map(
        per_device,
        mesh=mesh,
        in_specs=placed,
        out_specs=(P("expert", "tensor"), P("expert", "tensor"), P("expert", None)),
        check_vma=False,
    )
```

```python
import functools

import jax
import jax.numpy as jnp
from jax import lax
from jax.experimental import pallas as pl
from jax.experimental.pallas import tpu as pltpu
from jax.sharding import PartitionSpec as P

BF = jnp.bfloat16
F32 = jnp.float32


def dot(a, b, ca, cb):
    return lax.dot_general(a, b, (((ca,), (cb,)), ((), ())), preferred_element_type=F32)


def split2(v):
    hi = v.astype(BF).astype(F32)
    return hi, v - hi


def split3(v):
    hi, rest = split2(v)
    mid, low = split2(rest)
    return hi, mid, low


def route_maps(ids, probs, cap, slots):
    rows, top = ids.shape
    slot = lax.broadcasted_iota(jnp.int32, (rows, slots), 1)
    owner = slot // cap
    named = jnp.zeros((rows, slots), F32)
    weight = jnp.zeros((rows, slots), F32)
    for k in range(top):
        hit = ids[:, k : k + 1] == owner
        named = named + jnp.where(hit, 1.0, 0.0)
        weight = weight + jnp.where(hit, probs[:, k : k + 1], 0.0)
    before = (
        lax.broadcasted_iota(jnp.int32, (rows, rows), 0)
        > lax.broadcasted_iota(jnp.int32, (rows, rows), 1)
    ).astype(F32)
    rank = dot(before, named, 1, 0)
    fills = jnp.where(rank == (slot - owner * cap).astype(F32), named, 0.0)
    return fills, fills * weight, owner


def fetch(pairs, sems):
    copies = [pltpu.make_async_copy(s, d, sems.at[i]) for i, (s, d) in enumerate(pairs)]
    for c in copies:
        c.start()
    for c in copies:
        c.wait()


def send_kernel(cap, ids_hbm, probs_hbm, tok_hbm, grad_hbm, out, ids_ref, probs_ref, tok_ref, grad_ref, sems):
    fetch(
        ((ids_hbm, ids_ref), (probs_hbm, probs_ref), (tok_hbm, tok_ref), (grad_hbm, grad_ref)), sems
    )
    width = tok_ref.shape[1]
    fills, weighted, _ = route_maps(ids_ref[...], probs_ref[...], cap, out.shape[0])
    out[:, :width] = dot(fills.astype(BF), tok_ref[...], 0, 0).astype(BF)
    parts = jnp.concatenate(split3(weighted), axis=0).astype(BF)
    grad = grad_ref[...].astype(F32)
    thrice = jnp.concatenate([grad, grad, grad], axis=0).astype(BF)
    out[:, width:] = dot(parts, thrice, 0, 0).astype(BF)


def span(at_ref, offset, width):
    block = lax.rem(at_ref[0] + (8 + offset * at_ref[1]), 4)
    return pl.ds(pl.multiple_of(block * width, width), width)


def products(at_ref, block, offset, wg, wu, wd):
    width = block.shape[1] // 2
    s = span(at_ref, offset, width)
    x, g = block[:, :width], block[:, width:]
    return dot(x, wg[s, :], 1, 0), dot(x, wu[s, :], 1, 0), dot(g, wd[:, s], 1, 1)


def early_kernel(at_ref, own, near, wg_hbm, wu_hbm, wd_hbm, gate, up, hid, wg, wu, wd, sems):
    fetch(((wg_hbm, wg), (wu_hbm, wu), (wd_hbm, wd)), sems)
    ours, theirs = products(at_ref, own, 0, wg, wu, wd), products(at_ref, near, -1, wg, wu, wd)
    gate[...], up[...], hid[...] = [a + b for a, b in zip(ours, theirs)]


def partial_sums(at_ref, offset, o, hidden, grad_gate, grad_up, q_rows, wg, wu, wd):
    slots, width = hidden.shape[0], o.shape[1]
    s = span(at_ref, offset, width)
    o[:slots, :] = dot(hidden, wd[:, s], 1, 0).astype(BF)
    o[slots : 2 * slots, :] = (
        dot(grad_gate, wg[s, :], 1, 1) + dot(grad_up, wu[s, :], 1, 1)
    ).astype(BF)
    o[2 * slots :, :] = q_rows


def inner_kernel(at_ref, other, far, gate0, up0, hid0, wg, wu, wd, o, hidden_ref, gate_ref, up_ref, q_ref):
    gate, up, hid = gate0[...], up0[...], hid0[...]
    for block, offset in ((other, 1), (far, 2)):
        a, b, c = products(at_ref, block, offset, wg, wu, wd)
        gate, up, hid = gate + a, up + b, hid + c
    sig = 1.0 / (1.0 + jnp.exp(-gate))
    silu = gate * sig
    hidden = (silu * up).astype(BF)
    grad_gate = (hid * up * sig * (1.0 + gate * (1.0 - sig))).astype(BF)
    grad_up = (hid * silu).astype(BF)
    inner = jnp.concatenate(split3(hid * hidden.astype(F32)), axis=1).astype(BF)
    q_rows = q_pack(dot(jnp.ones((8, inner.shape[1]), BF), inner, 1, 1))
    hidden_ref[...], gate_ref[...], up_ref[...], q_ref[...] = hidden, grad_gate, grad_up, q_rows
    partial_sums(at_ref, 2, o, hidden, grad_gate, grad_up, q_rows, wg, wu, wd)


def outer_kernel(at_ref, hidden, grad_gate, grad_up, q_ref, wg, wu, wd, near, other, own):
    for offset, o in ((-1, other), (1, near), (0, own)):
        partial_sums(
            at_ref, offset, o, hidden[...], grad_gate[...], grad_up[...], q_ref[...], wg, wu, wd
        )


def q_pack(q):
    hi, low = split2(q)
    both = jnp.concatenate([hi, low], axis=1)
    return jnp.concatenate([both, both], axis=0).astype(BF)


def q_open(rows):
    both = rows.astype(F32)[:8]
    half = both.shape[1] // 2
    return both[:, :half] + both[:, half:]


def add_kernel(a, b, o):
    rows = a.shape[0] - 16
    o[:rows, :] = (a[:rows, :].astype(F32) + b[:rows, :].astype(F32)).astype(BF)
    o[rows:, :] = q_pack(q_open(a[rows:, :]) + q_open(b[rows:, :]))


def join_kernel(*refs):
    *parts, o = refs
    slots = o.shape[0]
    width = parts[0].shape[1]
    o[:, :width] = sum(r[:slots, :].astype(F32) for r in parts).astype(BF)
    o[:, width : 2 * width] = sum(r[slots : 2 * slots, :].astype(F32) for r in parts).astype(BF)
    hi, low = split2(sum(q_open(r[2 * slots :, :]) for r in parts))
    row = lax.broadcasted_iota(jnp.int32, hi.shape, 0)
    lines = jnp.where(row == 0, hi, jnp.where(row == 1, low, 0.0))
    lines = jnp.concatenate([lines, jnp.zeros((120, slots), F32)], axis=0).astype(BF)
    same = lax.broadcasted_iota(jnp.int32, (slots, slots), 0) == lax.broadcasted_iota(
        jnp.int32, (slots, slots), 1
    )
    o[:, 2 * width :] = dot(jnp.where(same, 1.0, 0.0).astype(BF), lines, 1, 1).astype(BF)


def mix_kernel(cap, ids_ref, probs_ref, got_ref, mixed_ref, grad_ref, prob_ref):
    ids, probs = ids_ref[...], probs_ref[...]
    rows, top = ids.shape
    width = mixed_ref.shape[1]
    fills, weighted, owner = route_maps(ids, probs, cap, got_ref.shape[0])
    parts = jnp.concatenate(split3(weighted), axis=0).astype(BF)
    sums = dot(parts, got_ref[:, :width], 1, 0)
    mixed_ref[...] = (sums[:rows] + sums[rows : 2 * rows] + sums[2 * rows :]).astype(BF)
    grad_ref[...] = dot(fills.astype(BF), got_ref[:, width : 2 * width], 1, 0).astype(BF)
    picks = [jnp.where(ids[:, k : k + 1] == owner, fills, 0.0) for k in range(top)]
    q = dot(jnp.concatenate(picks, axis=0).astype(BF), got_ref[:, 2 * width :], 1, 0)
    q = q[:, 0:1] + q[:, 1:2]
    place = lax.broadcasted_iota(jnp.int32, (rows, top), 1)
    result = jnp.zeros((rows, top), F32)
    for k in range(top):
        result = jnp.where(place == k, q[k * rows : (k + 1) * rows], result)
    prob_ref[...] = result / probs


VM = pl.BlockSpec(memory_space=pltpu.VMEM)
SM = pl.BlockSpec(memory_space=pltpu.SMEM)
HB = pl.BlockSpec(memory_space=pltpu.MemorySpace.HBM)


def stay(x):
    return pltpu.with_memory_space_constraint(x, pltpu.MemorySpace.HBM)


def call(kernel, args, outs, flops, specs=None, scratch=(), limit=8):
    moved = sum(a.size * a.dtype.itemsize for a in (*args, *outs))
    return pl.pallas_call(
        kernel,
        out_shape=outs,
        in_specs=specs or [VM] * len(args),
        out_specs=[VM] * len(outs),
        scratch_shapes=list(scratch),
        compiler_params=pltpu.CompilerParams(vmem_limit_bytes=limit << 20),
        cost_estimate=pl.CostEstimate(flops=flops, bytes_accessed=moved, transcendentals=0),
    )(*args)


def shift(x, d):
    pairs = []
    for e in range(lax.axis_size("expert")):
        way = d if e % 2 == 0 else -d
        pairs += [(e * 4 + t, e * 4 + (t + way) % 4) for t in range(4)]
    return lax.ppermute(x, ("expert", "tensor"), pairs)


def like(*arrays):
    return [pltpu.VMEM(a.shape, a.dtype) for a in arrays] + [pltpu.SemaphoreType.DMA((len(arrays),))]


def per_device(tokens, out_grad, expert_ids, gate_probs, w_gate, w_up, w_down):
    experts = lax.axis_size("expert")
    width = tokens.shape[1]
    hidden = w_gate.shape[2]
    cap = 2
    slots = experts * cap
    way = 1 - 2 * (lax.axis_index("expert") % 2)
    at = jnp.stack([lax.axis_index("tensor"), way]).astype(jnp.int32)

    def exchange(x):
        return lax.all_to_all(
            x.reshape(experts, cap, -1), "expert", split_axis=0, concat_axis=0, tiled=True
        )

    expert_ids, gate_probs = stay(expert_ids), stay(gate_probs)
    small = (expert_ids, gate_probs, stay(tokens), stay(out_grad))
    send, ids, probs = call(
        functools.partial(send_kernel, cap),
        small,
        (
            jax.ShapeDtypeStruct((slots, 2 * width), BF),
            jax.ShapeDtypeStruct(expert_ids.shape, jnp.int32),
            jax.ShapeDtypeStruct(gate_probs.shape, F32),
        ),
        2 * slots * width * 32,
        [HB] * 4,
        like(*small)[2:],
    )
    got = exchange(send)
    weights = (stay(w_gate[0]), stay(w_up[0]), stay(w_down[0]))
    work = 2 * slots * width * hidden * 24
    own = got.reshape(slots, 2 * width)
    near = shift(own, 1)
    again, near = lax.optimization_barrier((own, near))
    far = shift(near, 1)
    other = shift(again, -1)
    acc = jax.ShapeDtypeStruct((slots, hidden), F32)
    act = jax.ShapeDtypeStruct((slots, hidden), BF)
    piece = jax.ShapeDtypeStruct((2 * slots + 16, width), BF)
    held = [jax.ShapeDtypeStruct(w.shape, w.dtype) for w in weights]
    *first, wg, wu, wd = call(
        early_kernel,
        (at, own, near, *weights),
        (acc,) * 3 + tuple(held),
        work // 4,
        [SM, VM, VM] + [HB] * 3,
        [pltpu.SemaphoreType.DMA((3,))],
    )
    part_far, *kept = call(
        inner_kernel,
        (at, other, far, *first, wg, wu, wd),
        (piece, act, act, act, jax.ShapeDtypeStruct((16, width), BF)),
        work // 2,
        [SM] + [VM] * 8,
        limit=16,
    )
    via = shift(part_far, 1)
    part_near, part_other, part_own = call(
        outer_kernel, (at, *kept, wg, wu, wd), (piece,) * 3, 3 * work // 8, [SM] + [VM] * 7, limit=16
    )
    via, part_other = lax.optimization_barrier((via, part_other))
    from_other = shift(part_other, -1)
    (summed,) = call(add_kernel, (via, part_near), (piece,), slots * width)
    from_near = shift(summed, 1)
    (joined,) = call(
        join_kernel,
        (part_own, from_other, from_near),
        (jax.ShapeDtypeStruct((slots, 2 * width + 128), BF),),
        2 * slots * slots * 128,
    )
    back = exchange(joined)
    return call(
        functools.partial(mix_kernel, cap),
        (ids, probs, back.reshape(slots, -1)),
        (
            jax.ShapeDtypeStruct(tokens.shape, BF),
            jax.ShapeDtypeStruct(tokens.shape, BF),
            jax.ShapeDtypeStruct(gate_probs.shape, F32),
        ),
        2 * slots * width * 32,
    )


def solution(mesh):
    placed = (
        P("expert", "tensor"),
        P("expert", "tensor"),
        P("expert", None),
        P("expert", None),
        P("expert", None, "tensor"),
        P("expert", None, "tensor"),
        P("expert", "tensor", None),
    )
    return jax.shard_map(
        per_device,
        mesh=mesh,
        in_specs=placed,
        out_specs=(P("expert", "tensor"), P("expert", "tensor"), P("expert", None)),
        check_vma=False,
    )
```

```python
import functools

import jax
import jax.numpy as jnp
from jax import lax
from jax.experimental import pallas as pl
from jax.experimental.pallas import tpu as pltpu
from jax.sharding import PartitionSpec as P

BF = jnp.bfloat16
F32 = jnp.float32


def dot(a, b, ca, cb):
    return lax.dot_general(a, b, (((ca,), (cb,)), ((), ())), preferred_element_type=F32)


def split2(v):
    hi = v.astype(BF).astype(F32)
    return hi, v - hi


def split3(v):
    hi, rest = split2(v)
    mid, low = split2(rest)
    return hi, mid, low


def route_maps(ids, probs, cap, slots):
    rows, top = ids.shape
    slot = lax.broadcasted_iota(jnp.int32, (rows, slots), 1)
    owner = slot // cap
    named = jnp.zeros((rows, slots), F32)
    weight = jnp.zeros((rows, slots), F32)
    for k in range(top):
        hit = ids[:, k : k + 1] == owner
        named = named + jnp.where(hit, 1.0, 0.0)
        weight = weight + jnp.where(hit, probs[:, k : k + 1], 0.0)
    before = (
        lax.broadcasted_iota(jnp.int32, (rows, rows), 0)
        > lax.broadcasted_iota(jnp.int32, (rows, rows), 1)
    ).astype(F32)
    rank = dot(before, named, 1, 0)
    fills = jnp.where(rank == (slot - owner * cap).astype(F32), named, 0.0)
    return fills, fills * weight, owner


def fetch(pairs, sems):
    copies = [pltpu.make_async_copy(s, d, sems.at[i]) for i, (s, d) in enumerate(pairs)]
    for c in copies:
        c.start()
    for c in copies:
        c.wait()


def send_kernel(cap, ids_hbm, probs_hbm, tok_hbm, grad_hbm, out, ids_ref, probs_ref, tok_ref, grad_ref, sems):
    fetch(
        ((ids_hbm, ids_ref), (probs_hbm, probs_ref), (tok_hbm, tok_ref), (grad_hbm, grad_ref)), sems
    )
    width = tok_ref.shape[1]
    fills, weighted, _ = route_maps(ids_ref[...], probs_ref[...], cap, out.shape[0])
    out[:, :width] = dot(fills.astype(BF), tok_ref[...], 0, 0).astype(BF)
    parts = jnp.concatenate(split3(weighted), axis=0).astype(BF)
    grad = grad_ref[...].astype(F32)
    thrice = jnp.concatenate([grad, grad, grad], axis=0).astype(BF)
    out[:, width:] = dot(parts, thrice, 0, 0).astype(BF)


def span(at_ref, offset, width):
    block = lax.rem(at_ref[0] + (4 + offset), 4)
    return pl.ds(pl.multiple_of(block * width, width), width)


def products(at_ref, halves, offset, wg, wu, wd):
    both = [h[...] for h in halves]
    both = both[0] if len(both) == 1 else jnp.concatenate(both, axis=0)
    width = both.shape[1] // 2
    s = span(at_ref, offset, width)
    x, g = both[:, :width], both[:, width:]
    return dot(x, wg[s, :], 1, 0), dot(x, wu[s, :], 1, 0), dot(g, wd[:, s], 1, 1)


def load_kernel(turn, wg_hbm, wu_hbm, wd_hbm, wg, wu, wd, sems):
    fetch(((wg_hbm, wg), (wu_hbm, wu), (wd_hbm, wd)), sems)


def early_kernel(at_ref, own, left, r1, r2, wg, wu, wd, gate, up, hid):
    totals = products(at_ref, (own,), 0, wg, wu, wd)
    for halves, offset in (((left,), -1), ((r1, r2), 1)):
        totals = [t + p for t, p in zip(totals, products(at_ref, halves, offset, wg, wu, wd))]
    gate[...], up[...], hid[...] = totals


def partial_sums(at_ref, offset, forward, back, hidden, grad_gate, grad_up, q_rows, wg, wu, wd):
    slots, width = forward.shape
    s = span(at_ref, offset, width)
    forward[...] = dot(hidden, wd[:, s], 1, 0).astype(BF)
    back[:slots, :] = (dot(grad_gate, wg[s, :], 1, 1) + dot(grad_up, wu[s, :], 1, 1)).astype(BF)
    back[slots:, :] = q_rows


def inner_kernel(at_ref, f1, f2, gate0, up0, hid0, wg, wu, wd, forward, back, hidden_ref, gate_ref, up_ref, q_ref):
    gate, up, hid = [
        t[...] + p for t, p in zip((gate0, up0, hid0), products(at_ref, (f1, f2), 2, wg, wu, wd))
    ]
    sig = 1.0 / (1.0 + jnp.exp(-gate))
    silu = gate * sig
    hidden = (silu * up).astype(BF)
    grad_gate = (hid * up * sig * (1.0 + gate * (1.0 - sig))).astype(BF)
    grad_up = (hid * silu).astype(BF)
    inner = jnp.concatenate(split3(hid * hidden.astype(F32)), axis=1).astype(BF)
    q_rows = q_pack(dot(jnp.ones((8, inner.shape[1]), BF), inner, 1, 1))
    hidden_ref[...], gate_ref[...], up_ref[...], q_ref[...] = hidden, grad_gate, grad_up, q_rows
    partial_sums(at_ref, 2, forward, back, hidden, grad_gate, grad_up, q_rows, wg, wu, wd)


def outer_kernel(at_ref, hidden, grad_gate, grad_up, q_ref, wg, wu, wd, *outs):
    for i, offset in enumerate((-1, 1, 0)):
        partial_sums(
            at_ref, offset, outs[2 * i], outs[2 * i + 1], hidden[...], grad_gate[...], grad_up[...], q_ref[...], wg, wu, wd
        )


def q_pack(q):
    hi, low = split2(q)
    both = jnp.concatenate([hi, low], axis=1)
    return jnp.concatenate([both, both], axis=0).astype(BF)


def q_open(rows):
    both = rows.astype(F32)[:8]
    half = both.shape[1] // 2
    return both[:, :half] + both[:, half:]


def add_kernel(a, b, o):
    slots = a.shape[0] // 256 * 256
    o[:slots, :] = (a[:slots, :].astype(F32) + b[:slots, :].astype(F32)).astype(BF)
    o[slots:, :] = q_pack(q_open(a[slots:, :]) + q_open(b[slots:, :]))


def pair_kernel(a, b, direct, o):
    slots = a.shape[0]
    o[:slots, :] = (a[...].astype(F32) + b[...].astype(F32)).astype(BF)
    o[slots:, :] = direct[...]


def join_kernel(out_own, out_right, back_own, back_right, left, o):
    slots = o.shape[0]
    width = left.shape[1]
    fwd = (out_own[...], out_right[...], left[:slots, :])
    bwd = (back_own[...], back_right[...], left[slots:, :])
    o[:, :width] = sum(r.astype(F32) for r in fwd).astype(BF)
    o[:, width : 2 * width] = sum(r[:slots, :].astype(F32) for r in bwd).astype(BF)
    hi, low = split2(sum(q_open(r[slots:, :]) for r in bwd))
    row = lax.broadcasted_iota(jnp.int32, hi.shape, 0)
    lines = jnp.where(row == 0, hi, jnp.where(row == 1, low, 0.0))
    lines = jnp.concatenate([lines, jnp.zeros((120, slots), F32)], axis=0).astype(BF)
    same = lax.broadcasted_iota(jnp.int32, (slots, slots), 0) == lax.broadcasted_iota(
        jnp.int32, (slots, slots), 1
    )
    o[:, 2 * width :] = dot(jnp.where(same, 1.0, 0.0).astype(BF), lines, 1, 1).astype(BF)


def mix_kernel(cap, ids_ref, probs_ref, got_ref, mixed_ref, grad_ref, prob_ref):
    ids, probs = ids_ref[...], probs_ref[...]
    rows, top = ids.shape
    width = mixed_ref.shape[1]
    fills, weighted, owner = route_maps(ids, probs, cap, got_ref.shape[0])
    parts = jnp.concatenate(split3(weighted), axis=0).astype(BF)
    sums = dot(parts, got_ref[:, :width], 1, 0)
    mixed_ref[...] = (sums[:rows] + sums[rows : 2 * rows] + sums[2 * rows :]).astype(BF)
    grad_ref[...] = dot(fills.astype(BF), got_ref[:, width : 2 * width], 1, 0).astype(BF)
    picks = [jnp.where(ids[:, k : k + 1] == owner, fills, 0.0) for k in range(top)]
    q = dot(jnp.concatenate(picks, axis=0).astype(BF), got_ref[:, 2 * width :], 1, 0)
    q = q[:, 0:1] + q[:, 1:2]
    place = lax.broadcasted_iota(jnp.int32, (rows, top), 1)
    result = jnp.zeros((rows, top), F32)
    for k in range(top):
        result = jnp.where(place == k, q[k * rows : (k + 1) * rows], result)
    prob_ref[...] = result / probs


VM = pl.BlockSpec(memory_space=pltpu.VMEM)
SM = pl.BlockSpec(memory_space=pltpu.SMEM)
HB = pl.BlockSpec(memory_space=pltpu.MemorySpace.HBM)


def stay(x):
    return pltpu.with_memory_space_constraint(x, pltpu.MemorySpace.HBM)


def call(kernel, args, outs, flops, specs=None, scratch=(), limit=8):
    moved = sum(a.size * a.dtype.itemsize for a in (*args, *outs))
    return pl.pallas_call(
        kernel,
        out_shape=outs,
        in_specs=specs or [VM] * len(args),
        out_specs=[VM] * len(outs),
        scratch_shapes=list(scratch),
        compiler_params=pltpu.CompilerParams(vmem_limit_bytes=limit << 20),
        cost_estimate=pl.CostEstimate(flops=flops, bytes_accessed=moved, transcendentals=0),
    )(*args)


def shift(x, d):
    return lax.ppermute(x, "tensor", [(i, (i + d) % 4) for i in range(4)])


def like(*arrays):
    return [pltpu.VMEM(a.shape, a.dtype) for a in arrays] + [pltpu.SemaphoreType.DMA((len(arrays),))]


def per_device(tokens, out_grad, expert_ids, gate_probs, w_gate, w_up, w_down):
    experts = lax.axis_size("expert")
    width = tokens.shape[1]
    hidden = w_gate.shape[2]
    cap = 2
    slots = experts * cap
    at = lax.axis_index("tensor").astype(jnp.int32).reshape(1)

    def exchange(x):
        return lax.all_to_all(
            x.reshape(experts, cap, -1), "expert", split_axis=0, concat_axis=0, tiled=True
        )

    expert_ids, gate_probs = stay(expert_ids), stay(gate_probs)
    small = (expert_ids, gate_probs, stay(tokens), stay(out_grad))
    send, ids, probs = call(
        functools.partial(send_kernel, cap),
        small,
        (
            jax.ShapeDtypeStruct((slots, 2 * width), BF),
            jax.ShapeDtypeStruct(expert_ids.shape, jnp.int32),
            jax.ShapeDtypeStruct(gate_probs.shape, F32),
        ),
        2 * slots * width * 32,
        [HB] * 4,
        like(*small)[2:],
    )
    got = exchange(send)
    weights = (stay(w_gate[0]), stay(w_up[0]), stay(w_down[0]))
    work = 2 * slots * width * hidden * 24
    own = got.reshape(slots, 2 * width)
    half = slots // 2
    left = shift(own, 1)
    right_second, right_first = shift(own[half:], -1), shift(own[:half], -1)
    far_second, far_first = shift(right_second, -1), shift(left[:half], 1)
    acc = jax.ShapeDtypeStruct((slots, hidden), F32)
    table = jax.ShapeDtypeStruct((slots, width), BF)
    longer = jax.ShapeDtypeStruct((slots + 16, width), BF)
    held = [jax.ShapeDtypeStruct(w.shape, w.dtype) for w in weights]
    held = call(
        load_kernel,
        (right_second, *weights),
        held,
        work // 8,
        [VM] + [HB] * 3,
        [pltpu.SemaphoreType.DMA((3,))],
    )
    first = call(
        early_kernel,
        (at, own, left, right_first, right_second, *held),
        (acc,) * 3,
        3 * work // 8,
        [SM] + [VM] * 7,
        limit=16,
    )
    act = jax.ShapeDtypeStruct((slots, hidden), BF)
    out_far, back_far, *kept = call(
        inner_kernel,
        (at, far_first, far_second, *first, *held),
        (table, longer, act, act, act, jax.ShapeDtypeStruct((16, width), BF)),
        work // 4,
        [SM] + [VM] * 8,
        limit=16,
    )
    out_via, back_via = shift(out_far, 1), shift(back_far, -1)
    out_left, back_left, out_right, back_right, out_own, back_own = call(
        outer_kernel, (at, *kept, *held), (table, longer) * 3, 3 * work // 8, [SM] + [VM] * 7, limit=16
    )
    out_from_right = shift(out_left, -1)
    (to_right,) = call(
        pair_kernel,
        (out_via, out_right, back_right),
        (jax.ShapeDtypeStruct((2 * slots + 16, width), BF),),
        slots * width,
    )
    from_left = shift(to_right, 1)
    back_via, out_from_right = lax.optimization_barrier((back_via, out_from_right))
    (back_sum,) = call(add_kernel, (back_via, back_left), (longer,), slots * width)
    back_from_right = shift(back_sum, -1)
    (joined,) = call(
        join_kernel,
        (out_own, out_from_right, back_own, back_from_right, from_left),
        (jax.ShapeDtypeStruct((slots, 2 * width + 128), BF),),
        2 * slots * slots * 128,
    )
    back = exchange(joined)
    return call(
        functools.partial(mix_kernel, cap),
        (ids, probs, back.reshape(slots, -1)),
        (
            jax.ShapeDtypeStruct(tokens.shape, BF),
            jax.ShapeDtypeStruct(tokens.shape, BF),
            jax.ShapeDtypeStruct(gate_probs.shape, F32),
        ),
        2 * slots * width * 32,
    )


def solution(mesh):
    placed = (
        P("expert", "tensor"),
        P("expert", "tensor"),
        P("expert", None),
        P("expert", None),
        P("expert", None, "tensor"),
        P("expert", None, "tensor"),
        P("expert", "tensor", None),
    )
    return jax.shard_map(
        per_device,
        mesh=mesh,
        in_specs=placed,
        out_specs=(P("expert", "tensor"), P("expert", "tensor"), P("expert", None)),
        check_vma=False,
    )
```

```python
import functools

import jax
import jax.numpy as jnp
from jax import lax
from jax.experimental import pallas as pl
from jax.experimental.pallas import tpu as pltpu
from jax.sharding import PartitionSpec as P

BF = jnp.bfloat16
F32 = jnp.float32


def dot(a, b, ca, cb):
    return lax.dot_general(a, b, (((ca,), (cb,)), ((), ())), preferred_element_type=F32)


def split2(v):
    hi = v.astype(BF).astype(F32)
    return hi, v - hi


def split3(v):
    hi, rest = split2(v)
    mid, low = split2(rest)
    return hi, mid, low


def route_maps(ids, probs, cap, slots):
    rows, top = ids.shape
    slot = lax.broadcasted_iota(jnp.int32, (rows, slots), 1)
    owner = slot // cap
    named = jnp.zeros((rows, slots), F32)
    weight = jnp.zeros((rows, slots), F32)
    for k in range(top):
        hit = ids[:, k : k + 1] == owner
        named = named + jnp.where(hit, 1.0, 0.0)
        weight = weight + jnp.where(hit, probs[:, k : k + 1], 0.0)
    before = (
        lax.broadcasted_iota(jnp.int32, (rows, rows), 0)
        > lax.broadcasted_iota(jnp.int32, (rows, rows), 1)
    ).astype(F32)
    rank = dot(before, named, 1, 0)
    fills = jnp.where(rank == (slot - owner * cap).astype(F32), named, 0.0)
    return fills, fills * weight, owner


def fetch(pairs, sems):
    copies = [pltpu.make_async_copy(s, d, sems.at[i]) for i, (s, d) in enumerate(pairs)]
    for c in copies:
        c.start()
    for c in copies:
        c.wait()


def send_kernel(cap, ids_hbm, probs_hbm, tok_hbm, grad_hbm, out, ids_ref, probs_ref, tok_ref, grad_ref, sems):
    fetch(
        ((ids_hbm, ids_ref), (probs_hbm, probs_ref), (tok_hbm, tok_ref), (grad_hbm, grad_ref)), sems
    )
    width = tok_ref.shape[1]
    fills, weighted, _ = route_maps(ids_ref[...], probs_ref[...], cap, out.shape[0])
    out[:, :width] = dot(fills.astype(BF), tok_ref[...], 0, 0).astype(BF)
    parts = jnp.concatenate(split3(weighted), axis=0).astype(BF)
    grad = grad_ref[...].astype(F32)
    thrice = jnp.concatenate([grad, grad, grad], axis=0).astype(BF)
    out[:, width:] = dot(parts, thrice, 0, 0).astype(BF)


def span(at_ref, offset, width):
    block = lax.rem(at_ref[0] + (4 + offset), 4)
    return pl.ds(pl.multiple_of(block * width, width), width)


def products(at_ref, halves, offset, wg, wu, wd):
    both = jnp.concatenate([h[...] for h in halves], axis=0)
    width = both.shape[1] // 2
    s = span(at_ref, offset, width)
    x, g = both[:, :width], both[:, width:]
    return dot(x, wg[s, :], 1, 0), dot(x, wu[s, :], 1, 0), dot(g, wd[:, s], 1, 1)


def load_kernel(turn, wg_hbm, wu_hbm, wd_hbm, wg, wu, wd, sems):
    fetch(((wg_hbm, wg), (wu_hbm, wu), (wd_hbm, wd)), sems)


def early_kernel(at_ref, o1, o2, l1, l2, r1, r2, wg, wu, wd, gate, up, hid):
    totals = products(at_ref, (o1, o2), 0, wg, wu, wd)
    for halves, offset in (((l1, l2), -1), ((r1, r2), 1)):
        totals = [t + p for t, p in zip(totals, products(at_ref, halves, offset, wg, wu, wd))]
    gate[...], up[...], hid[...] = totals


def partial_sums(at_ref, offset, forward, back, hidden, grad_gate, grad_up, q_rows, wg, wu, wd):
    slots, width = forward.shape
    s = span(at_ref, offset, width)
    forward[...] = dot(hidden, wd[:, s], 1, 0).astype(BF)
    back[:slots, :] = (dot(grad_gate, wg[s, :], 1, 1) + dot(grad_up, wu[s, :], 1, 1)).astype(BF)
    back[slots:, :] = q_rows


def inner_kernel(at_ref, f1, f2, gate0, up0, hid0, wg, wu, wd, forward, back, hidden_ref, gate_ref, up_ref, q_ref):
    gate, up, hid = [
        t[...] + p for t, p in zip((gate0, up0, hid0), products(at_ref, (f1, f2), 2, wg, wu, wd))
    ]
    sig = 1.0 / (1.0 + jnp.exp(-gate))
    silu = gate * sig
    hidden = (silu * up).astype(BF)
    grad_gate = (hid * up * sig * (1.0 + gate * (1.0 - sig))).astype(BF)
    grad_up = (hid * silu).astype(BF)
    inner = jnp.concatenate(split3(hid * hidden.astype(F32)), axis=1).astype(BF)
    q_rows = q_pack(dot(jnp.ones((8, inner.shape[1]), BF), inner, 1, 1))
    hidden_ref[...], gate_ref[...], up_ref[...], q_ref[...] = hidden, grad_gate, grad_up, q_rows
    partial_sums(at_ref, 2, forward, back, hidden, grad_gate, grad_up, q_rows, wg, wu, wd)


def outer_kernel(at_ref, hidden, grad_gate, grad_up, q_ref, wg, wu, wd, *outs):
    for i, offset in enumerate((-1, 1, 0)):
        partial_sums(
            at_ref, offset, outs[2 * i], outs[2 * i + 1], hidden[...], grad_gate[...],
            grad_up[...], q_ref[...], wg, wu, wd
        )


def q_pack(q):
    hi, low = split2(q)
    both = jnp.concatenate([hi, low], axis=1)
    return jnp.concatenate([both, both], axis=0).astype(BF)


def q_open(rows):
    both = rows.astype(F32)[:8]
    half = both.shape[1] // 2
    return both[:, :half] + both[:, half:]


def add_kernel(a, b, o):
    slots = a.shape[0] // 256 * 256
    o[:slots, :] = (a[:slots, :].astype(F32) + b[:slots, :].astype(F32)).astype(BF)
    if slots < a.shape[0]:
        o[slots:, :] = q_pack(q_open(a[slots:, :]) + q_open(b[slots:, :]))


def join_kernel(*refs):
    fwd, bwd, o = refs[:3], refs[3:6], refs[6]
    slots = o.shape[0]
    width = fwd[0].shape[1]
    o[:, :width] = sum(r[...].astype(F32) for r in fwd).astype(BF)
    o[:, width : 2 * width] = sum(r[:slots, :].astype(F32) for r in bwd).astype(BF)
    hi, low = split2(sum(q_open(r[slots:, :]) for r in bwd))
    row = lax.broadcasted_iota(jnp.int32, hi.shape, 0)
    lines = jnp.where(row == 0, hi, jnp.where(row == 1, low, 0.0))
    lines = jnp.concatenate([lines, jnp.zeros((120, slots), F32)], axis=0).astype(BF)
    same = lax.broadcasted_iota(jnp.int32, (slots, slots), 0) == lax.broadcasted_iota(
        jnp.int32, (slots, slots), 1
    )
    o[:, 2 * width :] = dot(jnp.where(same, 1.0, 0.0).astype(BF), lines, 1, 1).astype(BF)


def mix_kernel(cap, ids_ref, probs_ref, got_ref, mixed_ref, grad_ref, prob_ref):
    ids, probs = ids_ref[...], probs_ref[...]
    rows, top = ids.shape
    width = mixed_ref.shape[1]
    fills, weighted, owner = route_maps(ids, probs, cap, got_ref.shape[0])
    parts = jnp.concatenate(split3(weighted), axis=0).astype(BF)
    sums = dot(parts, got_ref[:, :width], 1, 0)
    mixed_ref[...] = (sums[:rows] + sums[rows : 2 * rows] + sums[2 * rows :]).astype(BF)
    grad_ref[...] = dot(fills.astype(BF), got_ref[:, width : 2 * width], 1, 0).astype(BF)
    picks = [jnp.where(ids[:, k : k + 1] == owner, fills, 0.0) for k in range(top)]
    q = dot(jnp.concatenate(picks, axis=0).astype(BF), got_ref[:, 2 * width :], 1, 0)
    q = q[:, 0:1] + q[:, 1:2]
    place = lax.broadcasted_iota(jnp.int32, (rows, top), 1)
    result = jnp.zeros((rows, top), F32)
    for k in range(top):
        result = jnp.where(place == k, q[k * rows : (k + 1) * rows], result)
    prob_ref[...] = result / probs


VM = pl.BlockSpec(memory_space=pltpu.VMEM)
SM = pl.BlockSpec(memory_space=pltpu.SMEM)
HB = pl.BlockSpec(memory_space=pltpu.MemorySpace.HBM)


def stay(x):
    return pltpu.with_memory_space_constraint(x, pltpu.MemorySpace.HBM)


def call(kernel, args, outs, flops, specs=None, scratch=(), limit=8):
    moved = sum(a.size * a.dtype.itemsize for a in (*args, *outs))
    return pl.pallas_call(
        kernel,
        out_shape=outs,
        in_specs=specs or [VM] * len(args),
        out_specs=[VM] * len(outs),
        scratch_shapes=list(scratch),
        compiler_params=pltpu.CompilerParams(vmem_limit_bytes=limit << 20),
        cost_estimate=pl.CostEstimate(flops=flops, bytes_accessed=moved, transcendentals=0),
    )(*args)


def shift(x, d):
    return lax.ppermute(x, "tensor", [(i, (i + d) % 4) for i in range(4)])


def like(*arrays):
    return [pltpu.VMEM(a.shape, a.dtype) for a in arrays] + [pltpu.SemaphoreType.DMA((len(arrays),))]


def per_device(tokens, out_grad, expert_ids, gate_probs, w_gate, w_up, w_down):
    experts = lax.axis_size("expert")
    width = tokens.shape[1]
    hidden = w_gate.shape[2]
    cap = 2
    slots = experts * cap
    at = lax.axis_index("tensor").astype(jnp.int32).reshape(1)

    def exchange(x):
        return lax.all_to_all(
            x.reshape(experts, cap, -1), "expert", split_axis=0, concat_axis=0, tiled=True
        )

    expert_ids, gate_probs = stay(expert_ids), stay(gate_probs)
    small = (expert_ids, gate_probs, stay(tokens), stay(out_grad))
    send, ids, probs = call(
        functools.partial(send_kernel, cap),
        small,
        (
            jax.ShapeDtypeStruct((slots, 2 * width), BF),
            jax.ShapeDtypeStruct(expert_ids.shape, jnp.int32),
            jax.ShapeDtypeStruct(gate_probs.shape, F32),
        ),
        2 * slots * width * 32,
        [HB] * 4,
        like(*small)[2:],
    )
    got = exchange(send)
    weights = (stay(w_gate[0]), stay(w_up[0]), stay(w_down[0]))
    work = 2 * slots * width * hidden * 24
    first = got[: experts // 2].reshape(slots // 2, 2 * width)
    second = got[experts // 2 :].reshape(slots // 2, 2 * width)
    left_first, right_second = shift(first, 1), shift(second, -1)
    left_second, right_first = shift(second, 1), shift(first, -1)
    far_first, far_second = shift(left_first, 1), shift(right_second, -1)
    acc = jax.ShapeDtypeStruct((slots, hidden), F32)
    table = jax.ShapeDtypeStruct((slots, width), BF)
    longer = jax.ShapeDtypeStruct((slots + 16, width), BF)
    held = [jax.ShapeDtypeStruct(w.shape, w.dtype) for w in weights]
    held = call(
        load_kernel,
        (right_second, *weights),
        held,
        work // 8,
        [VM] + [HB] * 3,
        [pltpu.SemaphoreType.DMA((3,))],
    )
    known = call(
        early_kernel,
        (at, first, second, left_first, left_second, right_first, right_second, *held),
        (acc,) * 3,
        3 * work // 8,
        [SM] + [VM] * 9,
        limit=16,
    )
    act = jax.ShapeDtypeStruct((slots, hidden), BF)
    out_far, back_far, *kept = call(
        inner_kernel,
        (at, far_first, far_second, *known, *held),
        (table, longer, act, act, act, jax.ShapeDtypeStruct((16, width), BF)),
        work // 4,
        [SM] + [VM] * 8,
        limit=16,
    )
    out_via, back_via = shift(out_far, 1), shift(back_far, -1)
    out_left, back_left, out_right, back_right, out_own, back_own = call(
        outer_kernel, (at, *kept, *held), (table, longer) * 3, 3 * work // 8, [SM] + [VM] * 7, limit=16
    )
    back_from_left, out_from_right = shift(back_right, 1), shift(out_left, -1)
    (out_sum,) = call(add_kernel, (out_via, out_right), (table,), slots * width)
    (back_sum,) = call(add_kernel, (back_via, back_left), (longer,), slots * width)
    out_from_left, back_from_right = shift(out_sum, 1), shift(back_sum, -1)
    (joined,) = call(
        join_kernel,
        (out_own, out_from_left, out_from_right, back_own, back_from_left, back_from_right),
        (jax.ShapeDtypeStruct((slots, 2 * width + 128), BF),),
        2 * slots * slots * 128,
    )
    back = exchange(joined)
    return call(
        functools.partial(mix_kernel, cap),
        (ids, probs, back.reshape(slots, -1)),
        (
            jax.ShapeDtypeStruct(tokens.shape, BF),
            jax.ShapeDtypeStruct(tokens.shape, BF),
            jax.ShapeDtypeStruct(gate_probs.shape, F32),
        ),
        2 * slots * width * 32,
    )


def solution(mesh):
    placed = (
        P("expert", "tensor"),
        P("expert", "tensor"),
        P("expert", None),
        P("expert", None),
        P("expert", None, "tensor"),
        P("expert", None, "tensor"),
        P("expert", "tensor", None),
    )
    return jax.shard_map(
        per_device,
        mesh=mesh,
        in_specs=placed,
        out_specs=(P("expert", "tensor"), P("expert", "tensor"), P("expert", None)),
        check_vma=False,
    )
```

```python
import functools

import jax
import jax.numpy as jnp
from jax import lax
from jax.experimental import pallas as pl
from jax.experimental.pallas import tpu as pltpu
from jax.sharding import PartitionSpec as P

BF = jnp.bfloat16
F32 = jnp.float32


def dot(a, b, ca, cb):
    return lax.dot_general(a, b, (((ca,), (cb,)), ((), ())), preferred_element_type=F32)


def split2(v):
    hi = v.astype(BF).astype(F32)
    return hi, v - hi


def split3(v):
    hi, rest = split2(v)
    mid, low = split2(rest)
    return hi, mid, low


def route_maps(ids, probs, core, slots):
    rows, top = ids.shape
    slot = lax.broadcasted_iota(jnp.int32, (rows, slots), 1)
    owner = slot // 2 * 2 + core
    named = jnp.zeros((rows, slots), F32)
    weight = jnp.zeros((rows, slots), F32)
    for k in range(top):
        hit = ids[:, k : k + 1] == owner
        named = named + jnp.where(hit, 1.0, 0.0)
        weight = weight + jnp.where(hit, probs[:, k : k + 1], 0.0)
    before = (
        lax.broadcasted_iota(jnp.int32, (rows, rows), 0)
        > lax.broadcasted_iota(jnp.int32, (rows, rows), 1)
    ).astype(F32)
    rank = dot(before, named, 1, 0)
    fills = jnp.where(rank == (slot % 2).astype(F32), named, 0.0)
    return fills, fills * weight, owner


def fetch(pairs, sems):
    copies = [pltpu.make_async_copy(s, d, sems.at[i]) for i, (s, d) in enumerate(pairs)]
    for c in copies:
        c.start()
    for c in copies:
        c.wait()


def send_kernel(ids_hbm, probs_hbm, tok_hbm, grad_hbm, out, ids_ref, probs_ref, tok_ref, grad_ref, sems):
    fetch(
        ((ids_hbm, ids_ref), (probs_hbm, probs_ref), (tok_hbm, tok_ref), (grad_hbm, grad_ref)), sems
    )
    width = tok_ref.shape[1]
    grad = grad_ref[...].astype(F32)
    thrice = jnp.concatenate([grad, grad, grad], axis=0).astype(BF)
    for core in range(2):
        fills, weighted, _ = route_maps(ids_ref[...], probs_ref[...], core, out.shape[0])
        start = 2 * core * width
        out[:, start : start + width] = dot(fills.astype(BF), tok_ref[...], 0, 0).astype(BF)
        parts = jnp.concatenate(split3(weighted), axis=0).astype(BF)
        out[:, start + width : start + 2 * width] = dot(parts, thrice, 0, 0).astype(BF)


def spread_kernel(got, out):
    half = got.shape[1] // 2
    for core in range(2):
        for t in range(4):
            out[4 * core + t] = got[:, core * half : (core + 1) * half]


def expert_kernel(got, wg, wu, wd, out):
    width = got.shape[2] // 2
    half = got.shape[1]
    gate = up = hid = 0.0
    for t in range(4):
        s = slice(t * width, (t + 1) * width)
        both = jnp.concatenate([got[t], got[4 + t]], axis=0)
        x, g = both[:, :width], both[:, width:]
        gate = gate + dot(x, wg[s, :], 1, 0)
        up = up + dot(x, wu[s, :], 1, 0)
        hid = hid + dot(g, wd[:, s], 1, 1)
    sig = 1.0 / (1.0 + jnp.exp(-gate))
    silu = gate * sig
    hidden = (silu * up).astype(BF)
    grad_gate = (hid * up * sig * (1.0 + gate * (1.0 - sig))).astype(BF)
    grad_up = (hid * silu).astype(BF)
    inner = jnp.concatenate(split3(hid * hidden.astype(F32)), axis=1).astype(BF)
    q = dot(jnp.ones((8, inner.shape[1]), BF), inner, 1, 1)
    for t in range(4):
        s = slice(t * width, (t + 1) * width)
        forward = dot(hidden, wd[:, s], 1, 0).astype(BF)
        back = (dot(grad_gate, wg[s, :], 1, 1) + dot(grad_up, wu[s, :], 1, 1)).astype(BF)
        for core in range(2):
            rows = slice(core * half, (core + 1) * half)
            hi, low = split2(q[:, rows])
            line = jnp.concatenate([hi, low, hi * 0.0, hi * 0.0], axis=1)
            out[4 * core + t, :half, :] = forward[rows]
            out[4 * core + t, half : 2 * half, :] = back[rows]
            out[4 * core + t, 2 * half :, :] = jnp.concatenate([line, line], axis=0).astype(BF)


def join_kernel(got, out):
    half = out.shape[0]
    width = got.shape[2]
    step = 2 * width + 128
    for core in range(2):
        parts = [got[4 * core + t].astype(F32) for t in range(4)]
        total = parts[0] + parts[1] + parts[2] + parts[3]
        start = core * step
        out[:, start : start + width] = total[:half].astype(BF)
        out[:, start + width : start + 2 * width] = total[half : 2 * half].astype(BF)
        lines = total[2 * half : 2 * half + 8]
        hi, low = split2(lines[:, :half] + lines[:, half : 2 * half])
        row = lax.broadcasted_iota(jnp.int32, hi.shape, 0)
        lines = jnp.where(row == 0, hi, jnp.where(row == 1, low, 0.0))
        lines = jnp.concatenate([lines, jnp.zeros((120, half), F32)], axis=0).astype(BF)
        same = lax.broadcasted_iota(jnp.int32, (half, half), 0) == lax.broadcasted_iota(
            jnp.int32, (half, half), 1
        )
        turned = dot(jnp.where(same, 1.0, 0.0).astype(BF), lines, 1, 1).astype(BF)
        out[:, start + 2 * width : start + step] = turned


def mix_kernel(ids_ref, probs_ref, got_ref, mixed_ref, grad_ref, prob_ref):
    ids, probs = ids_ref[...], probs_ref[...]
    rows, top = ids.shape
    width = mixed_ref.shape[1]
    step = 2 * width + 128
    mixed = grad = q = 0.0
    for core in range(2):
        start = core * step
        fills, weighted, owner = route_maps(ids, probs, core, got_ref.shape[0])
        parts = jnp.concatenate(split3(weighted), axis=0).astype(BF)
        sums = dot(parts, got_ref[:, start : start + width], 1, 0)
        mixed = mixed + (sums[:rows] + sums[rows : 2 * rows] + sums[2 * rows :])
        grad = grad + dot(fills.astype(BF), got_ref[:, start + width : start + 2 * width], 1, 0)
        picks = [jnp.where(ids[:, k : k + 1] == owner, fills, 0.0) for k in range(top)]
        both = dot(
            jnp.concatenate(picks, axis=0).astype(BF),
            got_ref[:, start + 2 * width : start + step],
            1,
            0,
        )
        q = q + (both[:, 0:1] + both[:, 1:2])
    mixed_ref[...] = mixed.astype(BF)
    grad_ref[...] = grad.astype(BF)
    place = lax.broadcasted_iota(jnp.int32, (rows, top), 1)
    result = jnp.zeros((rows, top), F32)
    for k in range(top):
        result = jnp.where(place == k, q[k * rows : (k + 1) * rows], result)
    prob_ref[...] = result / probs


VM = pl.BlockSpec(memory_space=pltpu.VMEM)
HB = pl.BlockSpec(memory_space=pltpu.MemorySpace.HBM)


def stay(x):
    return pltpu.with_memory_space_constraint(x, pltpu.MemorySpace.HBM)


def call(kernel, args, outs, flops, specs=None, scratch=(), limit=12):
    moved = sum(a.size * a.dtype.itemsize for a in (*args, *outs))
    return pl.pallas_call(
        kernel,
        out_shape=outs,
        in_specs=specs or [VM] * len(args),
        out_specs=[VM] * len(outs),
        scratch_shapes=list(scratch),
        compiler_params=pltpu.CompilerParams(vmem_limit_bytes=limit << 20),
        cost_estimate=pl.CostEstimate(flops=flops, bytes_accessed=moved, transcendentals=0),
    )(*args)


def per_device(tokens, out_grad, expert_ids, gate_probs, w_gate, w_up, w_down):
    experts = lax.axis_size("expert")
    chips = experts // 2
    width = tokens.shape[1]
    hidden = w_gate.shape[2]
    rows = chips * 2
    same_core = [[2 * i + c for i in range(chips)] for c in range(2)]
    columns = [[8 * i + k for k in range(8)] for i in range(chips)]

    def across(x):
        y = x.reshape(chips, 2, -1)
        y = lax.all_to_all(y, "expert", 0, 0, tiled=True, axis_index_groups=same_core)
        return y.reshape(rows, -1)

    def column(x):
        return lax.all_to_all(
            x, ("expert", "tensor"), 0, 0, tiled=True, axis_index_groups=columns
        )

    small = [stay(x) for x in (expert_ids, gate_probs, tokens, out_grad)]
    send, ids, probs = call(
        send_kernel,
        small,
        (
            jax.ShapeDtypeStruct((rows, 4 * width), BF),
            jax.ShapeDtypeStruct(expert_ids.shape, jnp.int32),
            jax.ShapeDtypeStruct(gate_probs.shape, F32),
        ),
        4 * rows * width * 32,
        [HB] * 4,
        [pltpu.VMEM(x.shape, x.dtype) for x in small[2:]] + [pltpu.SemaphoreType.DMA((4,))],
    )
    got = across(send)
    work = 4 * rows * width * hidden * 24
    (spread,) = call(
        spread_kernel, (got,), (jax.ShapeDtypeStruct((8, rows, 2 * width), BF),), rows * width
    )
    (parts,) = call(
        expert_kernel,
        (column(spread), w_gate[0], w_up[0], w_down[0]),
        (jax.ShapeDtypeStruct((8, 2 * rows + 16, width), BF),),
        work,
        limit=20,
    )
    (joined,) = call(
        join_kernel,
        (column(parts),),
        (jax.ShapeDtypeStruct((rows, 4 * width + 256), BF),),
        2 * rows * rows * 256,
    )
    return call(
        mix_kernel,
        (ids, probs, across(joined)),
        (
            jax.ShapeDtypeStruct(tokens.shape, BF),
            jax.ShapeDtypeStruct(tokens.shape, BF),
            jax.ShapeDtypeStruct(gate_probs.shape, F32),
        ),
        4 * rows * width * 32,
    )


def solution(mesh):
    placed = (
        P("expert", "tensor"),
        P("expert", "tensor"),
        P("expert", None),
        P("expert", None),
        P("expert", None, "tensor"),
        P("expert", None, "tensor"),
        P("expert", "tensor", None),
    )
    return jax.shard_map(
        per_device,
        mesh=mesh,
        in_specs=placed,
        out_specs=(P("expert", "tensor"), P("expert", "tensor"), P("expert", None)),
        check_vma=False,
    )
```

```python
import functools

import jax
import jax.numpy as jnp
from jax import lax
from jax.experimental import pallas as pl
from jax.experimental.pallas import tpu as pltpu
from jax.sharding import PartitionSpec as P

BF = jnp.bfloat16
F32 = jnp.float32


def dot(a, b, ca, cb):
    return lax.dot_general(a, b, (((ca,), (cb,)), ((), ())), preferred_element_type=F32)


def split2(v):
    hi = v.astype(BF).astype(F32)
    return hi, v - hi


def split3(v):
    hi, rest = split2(v)
    mid, low = split2(rest)
    return hi, mid, low


def route_maps(ids, probs, core, slots):
    rows, top = ids.shape
    slot = lax.broadcasted_iota(jnp.int32, (rows, slots), 1)
    owner = slot // 2 * 2 + core
    named = jnp.zeros((rows, slots), F32)
    weight = jnp.zeros((rows, slots), F32)
    for k in range(top):
        hit = ids[:, k : k + 1] == owner
        named = named + jnp.where(hit, 1.0, 0.0)
        weight = weight + jnp.where(hit, probs[:, k : k + 1], 0.0)
    before = (
        lax.broadcasted_iota(jnp.int32, (rows, rows), 0)
        > lax.broadcasted_iota(jnp.int32, (rows, rows), 1)
    ).astype(F32)
    rank = dot(before, named, 1, 0)
    fills = jnp.where(rank == (slot % 2).astype(F32), named, 0.0)
    return fills, fills * weight, owner


def fetch(pairs, sems):
    copies = [pltpu.make_async_copy(s, d, sems.at[i]) for i, (s, d) in enumerate(pairs)]
    for c in copies:
        c.start()
    for c in copies:
        c.wait()


def send_kernel(core_ref, ids_hbm, probs_hbm, tok_hbm, grad_hbm, out, ids_ref, probs_ref, tok_ref, grad_ref, sems):
    fetch(
        ((ids_hbm, ids_ref), (probs_hbm, probs_ref), (tok_hbm, tok_ref), (grad_hbm, grad_ref)), sems
    )
    width = tok_ref.shape[1]
    grad = grad_ref[...].astype(F32)
    thrice = jnp.concatenate([grad, grad, grad], axis=0).astype(BF)
    for other in range(2):
        core = 1 - core_ref[0] if other else core_ref[0]
        fills, weighted, _ = route_maps(ids_ref[...], probs_ref[...], core, out.shape[0])
        start = 2 * other * width
        out[:, start : start + width] = dot(fills.astype(BF), tok_ref[...], 0, 0).astype(BF)
        parts = jnp.concatenate(split3(weighted), axis=0).astype(BF)
        out[:, start + width : start + 2 * width] = dot(parts, thrice, 0, 0).astype(BF)


def span(at_ref, offset, width):
    block = lax.rem(at_ref[0] + (4 + offset), 4)
    return pl.ds(pl.multiple_of(block * width, width), width)


def products(at_ref, halves, offset, wg, wu, wd):
    both = jnp.concatenate([h[...] for h in halves], axis=0)
    width = both.shape[1] // 2
    s = span(at_ref, offset, width)
    x, g = both[:, :width], both[:, width:]
    return dot(x, wg[s, :], 1, 0), dot(x, wu[s, :], 1, 0), dot(g, wd[:, s], 1, 1)


def load_kernel(turn, wg_hbm, wu_hbm, wd_hbm, wg, wu, wd, sems):
    fetch(((wg_hbm, wg), (wu_hbm, wu), (wd_hbm, wd)), sems)


def early_kernel(at_ref, o1, o2, l1, l2, r1, r2, wg, wu, wd, gate, up, hid):
    totals = products(at_ref, (o1, o2), 0, wg, wu, wd)
    for halves, offset in (((l1, l2), -1), ((r1, r2), 1)):
        totals = [t + p for t, p in zip(totals, products(at_ref, halves, offset, wg, wu, wd))]
    gate[...], up[...], hid[...] = totals


def partial_sums(at_ref, offset, ours, theirs, hidden, grad_gate, grad_up, q_rows, wg, wu, wd):
    half, width = hidden.shape[0] // 2, ours.shape[1]
    s = span(at_ref, offset, width)
    forward = dot(hidden, wd[:, s], 1, 0).astype(BF)
    back = (dot(grad_gate, wg[s, :], 1, 1) + dot(grad_up, wu[s, :], 1, 1)).astype(BF)
    for i, o in enumerate((ours, theirs)):
        o[:half, :] = forward[i * half : (i + 1) * half]
        o[half : 2 * half, :] = back[i * half : (i + 1) * half]
        o[2 * half :, :] = q_rows[16 * i : 16 * i + 16]


def inner_kernel(at_ref, f1, f2, gate0, up0, hid0, wg, wu, wd, ours, theirs, hidden_ref, gate_ref, up_ref, q_ref):
    gate, up, hid = [
        t[...] + p for t, p in zip((gate0, up0, hid0), products(at_ref, (f1, f2), 2, wg, wu, wd))
    ]
    sig = 1.0 / (1.0 + jnp.exp(-gate))
    silu = gate * sig
    hidden = (silu * up).astype(BF)
    grad_gate = (hid * up * sig * (1.0 + gate * (1.0 - sig))).astype(BF)
    grad_up = (hid * silu).astype(BF)
    inner = jnp.concatenate(split3(hid * hidden.astype(F32)), axis=1).astype(BF)
    q = dot(jnp.ones((8, inner.shape[1]), BF), inner, 1, 1)
    half = hidden.shape[0] // 2
    q_rows = jnp.concatenate([q_pack(q[:, :half]), q_pack(q[:, half:])], axis=0)
    hidden_ref[...], gate_ref[...], up_ref[...], q_ref[...] = hidden, grad_gate, grad_up, q_rows
    partial_sums(at_ref, 2, ours, theirs, hidden, grad_gate, grad_up, q_rows, wg, wu, wd)


def outer_kernel(at_ref, hidden, grad_gate, grad_up, q_ref, wg, wu, wd, *outs):
    for i, offset in enumerate((-1, 1, 0)):
        partial_sums(
            at_ref, offset, outs[2 * i], outs[2 * i + 1], hidden[...], grad_gate[...],
            grad_up[...], q_ref[...], wg, wu, wd
        )


def q_pack(q):
    hi, low = split2(q)
    both = jnp.concatenate([hi, low, jnp.zeros((8, 256), F32)], axis=1)
    return jnp.concatenate([both, both], axis=0).astype(BF)


def q_open(rows):
    both = rows.astype(F32)[:8]
    return both[:, :128] + both[:, 128:256]


def add_kernel(a, b, o):
    rows = a.shape[0] - 16
    o[:rows, :] = (a[:rows, :].astype(F32) + b[:rows, :].astype(F32)).astype(BF)
    o[rows:, :] = q_pack(q_open(a[rows:, :]) + q_open(b[rows:, :]))


def join_kernel(*refs):
    out = refs[6]
    half = out.shape[0]
    width = refs[0].shape[1]
    step = 2 * width + 128
    for i in range(2):
        parts = refs[3 * i : 3 * i + 3]
        total = sum(r[: 2 * half, :].astype(F32) for r in parts)
        start = i * step
        out[:, start : start + width] = total[:half].astype(BF)
        out[:, start + width : start + 2 * width] = total[half:].astype(BF)
        hi, low = split2(sum(q_open(r[2 * half :, :]) for r in parts))
        row = lax.broadcasted_iota(jnp.int32, hi.shape, 0)
        lines = jnp.where(row == 0, hi, jnp.where(row == 1, low, 0.0))
        lines = jnp.concatenate([lines, jnp.zeros((120, half), F32)], axis=0).astype(BF)
        same = lax.broadcasted_iota(jnp.int32, (half, half), 0) == lax.broadcasted_iota(
            jnp.int32, (half, half), 1
        )
        turned = dot(jnp.where(same, 1.0, 0.0).astype(BF), lines, 1, 1).astype(BF)
        out[:, start + 2 * width : start + step] = turned


def mix_kernel(core_ref, ids_ref, probs_ref, got_ref, mixed_ref, grad_ref, prob_ref):
    ids, probs = ids_ref[...], probs_ref[...]
    rows, top = ids.shape
    width = mixed_ref.shape[1]
    step = 2 * width + 128
    mixed = grad = q = 0.0
    for other in range(2):
        core = 1 - core_ref[0] if other else core_ref[0]
        start = other * step
        fills, weighted, owner = route_maps(ids, probs, core, got_ref.shape[0])
        parts = jnp.concatenate(split3(weighted), axis=0).astype(BF)
        sums = dot(parts, got_ref[:, start : start + width], 1, 0)
        mixed = mixed + (sums[:rows] + sums[rows : 2 * rows] + sums[2 * rows :])
        grad = grad + dot(fills.astype(BF), got_ref[:, start + width : start + 2 * width], 1, 0)
        picks = [jnp.where(ids[:, k : k + 1] == owner, fills, 0.0) for k in range(top)]
        both = dot(
            jnp.concatenate(picks, axis=0).astype(BF),
            got_ref[:, start + 2 * width : start + step],
            1,
            0,
        )
        q = q + (both[:, 0:1] + both[:, 1:2])
    mixed_ref[...] = mixed.astype(BF)
    grad_ref[...] = grad.astype(BF)
    place = lax.broadcasted_iota(jnp.int32, (rows, top), 1)
    result = jnp.zeros((rows, top), F32)
    for k in range(top):
        result = jnp.where(place == k, q[k * rows : (k + 1) * rows], result)
    prob_ref[...] = result / probs


VM = pl.BlockSpec(memory_space=pltpu.VMEM)
SM = pl.BlockSpec(memory_space=pltpu.SMEM)
HB = pl.BlockSpec(memory_space=pltpu.MemorySpace.HBM)


def stay(x):
    return pltpu.with_memory_space_constraint(x, pltpu.MemorySpace.HBM)


def call(kernel, args, outs, flops, specs=None, scratch=(), limit=12):
    moved = sum(a.size * a.dtype.itemsize for a in (*args, *outs))
    return pl.pallas_call(
        kernel,
        out_shape=outs,
        in_specs=specs or [VM] * len(args),
        out_specs=[VM] * len(outs),
        scratch_shapes=list(scratch),
        compiler_params=pltpu.CompilerParams(vmem_limit_bytes=limit << 20),
        cost_estimate=pl.CostEstimate(flops=flops, bytes_accessed=moved, transcendentals=0),
    )(*args)


def per_device(tokens, out_grad, expert_ids, gate_probs, w_gate, w_up, w_down):
    experts = lax.axis_size("expert")
    chips = experts // 2
    width = tokens.shape[1]
    hidden = w_gate.shape[2]
    rows = chips * 2
    same_core = [[2 * i + c for i in range(chips)] for c in range(2)]

    def across(x):
        y = x.reshape(chips, 2, -1)
        y = lax.all_to_all(y, "expert", 0, 0, tiled=True, axis_index_groups=same_core)
        return y.reshape(rows, -1)

    def shift(x, d, cross=0):
        pairs = [
            (e * 4 + t, (e ^ cross) * 4 + (t + d) % 4) for e in range(experts) for t in range(4)
        ]
        return lax.ppermute(x, ("expert", "tensor"), pairs)

    at = lax.axis_index("tensor").astype(jnp.int32).reshape(1)
    core = (lax.axis_index("expert") % 2).astype(jnp.int32).reshape(1)
    small = [stay(x) for x in (expert_ids, gate_probs, tokens, out_grad)]
    send, ids, probs = call(
        send_kernel,
        (core, *small),
        (
            jax.ShapeDtypeStruct((rows, 4 * width), BF),
            jax.ShapeDtypeStruct(expert_ids.shape, jnp.int32),
            jax.ShapeDtypeStruct(gate_probs.shape, F32),
        ),
        4 * rows * width * 32,
        [SM] + [HB] * 4,
        [pltpu.VMEM(x.shape, x.dtype) for x in small[2:]] + [pltpu.SemaphoreType.DMA((4,))],
    )
    got = across(send).reshape(chips, 2, -1)
    ours = got[:, :, : 2 * width].reshape(rows, 2 * width)
    theirs = got[:, :, 2 * width :].reshape(rows, 2 * width)
    left_ours, right_theirs = shift(ours, 1), shift(theirs, -1, 1)
    left_theirs, right_ours = shift(theirs, 1, 1), shift(ours, -1)
    theirs, left_ours, right_theirs = lax.optimization_barrier((theirs, left_ours, right_theirs))
    far_ours, far_theirs = shift(left_ours, 1), shift(right_theirs, -1)
    own_theirs = shift(theirs, 0, 1)
    slots = 2 * rows
    weights = [stay(w[0]) for w in (w_gate, w_up, w_down)]
    work = 4 * rows * width * hidden * 24
    acc = jax.ShapeDtypeStruct((slots, hidden), F32)
    act = jax.ShapeDtypeStruct((slots, hidden), BF)
    piece = jax.ShapeDtypeStruct((slots + 16, width), BF)
    held = call(
        load_kernel,
        (right_theirs, *weights),
        [jax.ShapeDtypeStruct(w.shape, w.dtype) for w in weights],
        work // 8,
        [VM] + [HB] * 3,
        [pltpu.SemaphoreType.DMA((3,))],
    )
    known = call(
        early_kernel,
        (at, ours, own_theirs, left_ours, left_theirs, right_ours, right_theirs, *held),
        (acc,) * 3,
        3 * work // 8,
        [SM] + [VM] * 9,
        limit=16,
    )
    a_far, b_far, *kept = call(
        inner_kernel,
        (at, far_ours, far_theirs, *known, *held),
        (piece, piece, act, act, act, jax.ShapeDtypeStruct((32, width), BF)),
        work // 4,
        [SM] + [VM] * 8,
        limit=16,
    )
    a_via, b_via = shift(a_far, 1), shift(b_far, -1)
    a_left, b_left, a_right, b_right, a_own, b_own = call(
        outer_kernel, (at, *kept, *held), (piece,) * 6, 3 * work // 8, [SM] + [VM] * 7, limit=16
    )
    b_from_left, a_from_right = shift(b_right, 1, 1), shift(a_left, -1)
    (a_sum,) = call(add_kernel, (a_via, a_right), (piece,), slots * width)
    (b_sum,) = call(add_kernel, (b_via, b_left), (piece,), slots * width)
    a_sum, b_own = lax.optimization_barrier((a_sum, b_own))
    a_from_left, b_from_right = shift(a_sum, 1), shift(b_sum, -1, 1)
    b_here = shift(b_own, 0, 1)
    (joined,) = call(
        join_kernel,
        (a_own, a_from_left, a_from_right, b_here, b_from_left, b_from_right),
        (jax.ShapeDtypeStruct((rows, 4 * width + 256), BF),),
        2 * rows * rows * 256,
    )
    return call(
        mix_kernel,
        (core, ids, probs, across(joined)),
        (
            jax.ShapeDtypeStruct(tokens.shape, BF),
            jax.ShapeDtypeStruct(tokens.shape, BF),
            jax.ShapeDtypeStruct(gate_probs.shape, F32),
        ),
        4 * rows * width * 32,
        [SM] + [VM] * 3,
    )


def solution(mesh):
    placed = (
        P("expert", "tensor"),
        P("expert", "tensor"),
        P("expert", None),
        P("expert", None),
        P("expert", None, "tensor"),
        P("expert", None, "tensor"),
        P("expert", "tensor", None),
    )
    return jax.shard_map(
        per_device,
        mesh=mesh,
        in_specs=placed,
        out_specs=(P("expert", "tensor"), P("expert", "tensor"), P("expert", None)),
        check_vma=False,
    )
```

```python
import functools

import jax
import jax.numpy as jnp
from jax import lax
from jax.experimental import pallas as pl
from jax.experimental.pallas import tpu as pltpu
from jax.sharding import PartitionSpec as P

BF = jnp.bfloat16
F32 = jnp.float32


def dot(a, b, ca, cb):
    return lax.dot_general(a, b, (((ca,), (cb,)), ((), ())), preferred_element_type=F32)


def split2(v):
    hi = v.astype(BF).astype(F32)
    return hi, v - hi


def split3(v):
    hi, rest = split2(v)
    mid, low = split2(rest)
    return hi, mid, low


def route_maps(ids, probs, cap, slots):
    rows, top = ids.shape
    slot = lax.broadcasted_iota(jnp.int32, (rows, slots), 1)
    owner = slot // cap
    named = jnp.zeros((rows, slots), F32)
    weight = jnp.zeros((rows, slots), F32)
    for k in range(top):
        hit = ids[:, k : k + 1] == owner
        named = named + jnp.where(hit, 1.0, 0.0)
        weight = weight + jnp.where(hit, probs[:, k : k + 1], 0.0)
    before = (
        lax.broadcasted_iota(jnp.int32, (rows, rows), 0)
        > lax.broadcasted_iota(jnp.int32, (rows, rows), 1)
    ).astype(F32)
    rank = dot(before, named, 1, 0)
    fills = jnp.where(rank == (slot - owner * cap).astype(F32), named, 0.0)
    return fills, fills * weight, owner


def fetch(pairs, sems):
    copies = [pltpu.make_async_copy(s, d, sems.at[i]) for i, (s, d) in enumerate(pairs)]
    for c in copies:
        c.start()
    for c in copies:
        c.wait()


def send_kernel(cap, ids_hbm, probs_hbm, tok_hbm, grad_hbm, out, ids_ref, probs_ref, tok_ref, grad_ref, sems):
    fetch(
        ((ids_hbm, ids_ref), (probs_hbm, probs_ref), (tok_hbm, tok_ref), (grad_hbm, grad_ref)), sems
    )
    width = tok_ref.shape[1]
    fills, weighted, _ = route_maps(ids_ref[...], probs_ref[...], cap, out.shape[0])
    out[:, :width] = dot(fills.astype(BF), tok_ref[...], 0, 0).astype(BF)
    parts = jnp.concatenate(split3(weighted), axis=0).astype(BF)
    grad = grad_ref[...].astype(F32)
    thrice = jnp.concatenate([grad, grad, grad], axis=0).astype(BF)
    out[:, width:] = dot(parts, thrice, 0, 0).astype(BF)


def span(at_ref, offset, width):
    block = lax.rem(at_ref[0] + (8 + offset * at_ref[1]), 4)
    return pl.ds(pl.multiple_of(block * width, width), width)


def products(at_ref, halves, offset, wg, wu, wd):
    both = jnp.concatenate([h[...] for h in halves], axis=0)
    width = both.shape[1] // 2
    s = span(at_ref, offset, width)
    x, g = both[:, :width], both[:, width:]
    return dot(x, wg[s, :], 1, 0), dot(x, wu[s, :], 1, 0), dot(g, wd[:, s], 1, 1)


def load_kernel(turn, wg_hbm, wu_hbm, wd_hbm, wg, wu, wd, sems):
    fetch(((wg_hbm, wg), (wu_hbm, wu), (wd_hbm, wd)), sems)


def early_kernel(at_ref, o1, o2, l1, l2, r1, r2, wg, wu, wd, gate, up, hid):
    totals = products(at_ref, (o1, o2), 0, wg, wu, wd)
    for halves, offset in (((l1, l2), -1), ((r1, r2), 1)):
        totals = [t + p for t, p in zip(totals, products(at_ref, halves, offset, wg, wu, wd))]
    gate[...], up[...], hid[...] = totals


def partial_sums(at_ref, offset, forward, back, hidden, grad_gate, grad_up, q_rows, wg, wu, wd):
    slots, width = forward.shape
    s = span(at_ref, offset, width)
    forward[...] = dot(hidden, wd[:, s], 1, 0).astype(BF)
    back[:slots, :] = (dot(grad_gate, wg[s, :], 1, 1) + dot(grad_up, wu[s, :], 1, 1)).astype(BF)
    back[slots:, :] = q_rows


def inner_kernel(at_ref, f1, f2, gate0, up0, hid0, wg, wu, wd, forward, back, hidden_ref, gate_ref, up_ref, q_ref):
    gate, up, hid = [
        t[...] + p for t, p in zip((gate0, up0, hid0), products(at_ref, (f1, f2), 2, wg, wu, wd))
    ]
    sig = 1.0 / (1.0 + jnp.exp(-gate))
    silu = gate * sig
    hidden = (silu * up).astype(BF)
    grad_gate = (hid * up * sig * (1.0 + gate * (1.0 - sig))).astype(BF)
    grad_up = (hid * silu).astype(BF)
    inner = jnp.concatenate(split3(hid * hidden.astype(F32)), axis=1).astype(BF)
    q_rows = q_pack(dot(jnp.ones((8, inner.shape[1]), BF), inner, 1, 1))
    hidden_ref[...], gate_ref[...], up_ref[...], q_ref[...] = hidden, grad_gate, grad_up, q_rows
    partial_sums(at_ref, 2, forward, back, hidden, grad_gate, grad_up, q_rows, wg, wu, wd)


def outer_kernel(at_ref, hidden, grad_gate, grad_up, q_ref, wg, wu, wd, *outs):
    for i, offset in enumerate((-1, 1, 0)):
        partial_sums(
            at_ref, offset, outs[2 * i], outs[2 * i + 1], hidden[...], grad_gate[...],
            grad_up[...], q_ref[...], wg, wu, wd
        )


def q_pack(q):
    hi, low = split2(q)
    both = jnp.concatenate([hi, low], axis=1)
    return jnp.concatenate([both, both], axis=0).astype(BF)


def q_open(rows):
    both = rows.astype(F32)[:8]
    half = both.shape[1] // 2
    return both[:, :half] + both[:, half:]


def add_kernel(a, b, o):
    slots = a.shape[0] // 256 * 256
    o[:slots, :] = (a[:slots, :].astype(F32) + b[:slots, :].astype(F32)).astype(BF)
    if slots < a.shape[0]:
        o[slots:, :] = q_pack(q_open(a[slots:, :]) + q_open(b[slots:, :]))


def join_kernel(*refs):
    fwd, bwd, o = refs[:3], refs[3:6], refs[6]
    slots = o.shape[0]
    width = fwd[0].shape[1]
    o[:, :width] = sum(r[...].astype(F32) for r in fwd).astype(BF)
    o[:, width : 2 * width] = sum(r[:slots, :].astype(F32) for r in bwd).astype(BF)
    hi, low = split2(sum(q_open(r[slots:, :]) for r in bwd))
    row = lax.broadcasted_iota(jnp.int32, hi.shape, 0)
    lines = jnp.where(row == 0, hi, jnp.where(row == 1, low, 0.0))
    lines = jnp.concatenate([lines, jnp.zeros((120, slots), F32)], axis=0).astype(BF)
    same = lax.broadcasted_iota(jnp.int32, (slots, slots), 0) == lax.broadcasted_iota(
        jnp.int32, (slots, slots), 1
    )
    o[:, 2 * width :] = dot(jnp.where(same, 1.0, 0.0).astype(BF), lines, 1, 1).astype(BF)


def mix_kernel(cap, ids_ref, probs_ref, got_ref, mixed_ref, grad_ref, prob_ref):
    ids, probs = ids_ref[...], probs_ref[...]
    rows, top = ids.shape
    width = mixed_ref.shape[1]
    fills, weighted, owner = route_maps(ids, probs, cap, got_ref.shape[0])
    parts = jnp.concatenate(split3(weighted), axis=0).astype(BF)
    sums = dot(parts, got_ref[:, :width], 1, 0)
    mixed_ref[...] = (sums[:rows] + sums[rows : 2 * rows] + sums[2 * rows :]).astype(BF)
    grad_ref[...] = dot(fills.astype(BF), got_ref[:, width : 2 * width], 1, 0).astype(BF)
    picks = [jnp.where(ids[:, k : k + 1] == owner, fills, 0.0) for k in range(top)]
    q = dot(jnp.concatenate(picks, axis=0).astype(BF), got_ref[:, 2 * width :], 1, 0)
    q = q[:, 0:1] + q[:, 1:2]
    place = lax.broadcasted_iota(jnp.int32, (rows, top), 1)
    result = jnp.zeros((rows, top), F32)
    for k in range(top):
        result = jnp.where(place == k, q[k * rows : (k + 1) * rows], result)
    prob_ref[...] = result / probs


VM = pl.BlockSpec(memory_space=pltpu.VMEM)
SM = pl.BlockSpec(memory_space=pltpu.SMEM)
HB = pl.BlockSpec(memory_space=pltpu.MemorySpace.HBM)


def stay(x):
    return pltpu.with_memory_space_constraint(x, pltpu.MemorySpace.HBM)


def call(kernel, args, outs, flops, specs=None, scratch=(), limit=8):
    moved = sum(a.size * a.dtype.itemsize for a in (*args, *outs))
    return pl.pallas_call(
        kernel,
        out_shape=outs,
        in_specs=specs or [VM] * len(args),
        out_specs=[VM] * len(outs),
        scratch_shapes=list(scratch),
        compiler_params=pltpu.CompilerParams(vmem_limit_bytes=limit << 20),
        cost_estimate=pl.CostEstimate(flops=flops, bytes_accessed=moved, transcendentals=0),
    )(*args)


def shift(x, d):
    pairs = []
    for e in range(lax.axis_size("expert")):
        way = d if e % 2 == 0 else -d
        pairs += [(e * 4 + t, e * 4 + (t + way) % 4) for t in range(4)]
    return lax.ppermute(x, ("expert", "tensor"), pairs)


def like(*arrays):
    return [pltpu.VMEM(a.shape, a.dtype) for a in arrays] + [pltpu.SemaphoreType.DMA((len(arrays),))]


def per_device(tokens, out_grad, expert_ids, gate_probs, w_gate, w_up, w_down):
    experts = lax.axis_size("expert")
    width = tokens.shape[1]
    hidden = w_gate.shape[2]
    cap = 2
    slots = experts * cap
    way = 1 - 2 * (lax.axis_index("expert") % 2)
    at = jnp.stack([lax.axis_index("tensor"), way]).astype(jnp.int32)

    def exchange(x):
        return lax.all_to_all(
            x.reshape(experts, cap, -1), "expert", split_axis=0, concat_axis=0, tiled=True
        )

    expert_ids, gate_probs = stay(expert_ids), stay(gate_probs)
    small = (expert_ids, gate_probs, stay(tokens), stay(out_grad))
    send, ids, probs = call(
        functools.partial(send_kernel, cap),
        small,
        (
            jax.ShapeDtypeStruct((slots, 2 * width), BF),
            jax.ShapeDtypeStruct(expert_ids.shape, jnp.int32),
            jax.ShapeDtypeStruct(gate_probs.shape, F32),
        ),
        2 * slots * width * 32,
        [HB] * 4,
        like(*small)[2:],
    )
    got = exchange(send)
    weights = (stay(w_gate[0]), stay(w_up[0]), stay(w_down[0]))
    work = 2 * slots * width * hidden * 24
    first = got[: experts // 2].reshape(slots // 2, 2 * width)
    second = got[experts // 2 :].reshape(slots // 2, 2 * width)
    left_first, right_second = shift(first, 1), shift(second, -1)
    left_second, right_first = shift(second, 1), shift(first, -1)
    far_first, far_second = shift(left_first, 1), shift(right_second, -1)
    acc = jax.ShapeDtypeStruct((slots, hidden), F32)
    table = jax.ShapeDtypeStruct((slots, width), BF)
    longer = jax.ShapeDtypeStruct((slots + 16, width), BF)
    held = [jax.ShapeDtypeStruct(w.shape, w.dtype) for w in weights]
    held = call(
        load_kernel,
        (right_second, *weights),
        held,
        work // 8,
        [VM] + [HB] * 3,
        [pltpu.SemaphoreType.DMA((3,))],
    )
    known = call(
        early_kernel,
        (at, first, second, left_first, left_second, right_first, right_second, *held),
        (acc,) * 3,
        3 * work // 8,
        [SM] + [VM] * 9,
        limit=16,
    )
    act = jax.ShapeDtypeStruct((slots, hidden), BF)
    out_far, back_far, *kept = call(
        inner_kernel,
        (at, far_first, far_second, *known, *held),
        (table, longer, act, act, act, jax.ShapeDtypeStruct((16, width), BF)),
        work // 4,
        [SM] + [VM] * 8,
        limit=16,
    )
    out_via, back_via = shift(out_far, 1), shift(back_far, -1)
    out_left, back_left, out_right, back_right, out_own, back_own = call(
        outer_kernel, (at, *kept, *held), (table, longer) * 3, 3 * work // 8, [SM] + [VM] * 7, limit=16
    )
    back_from_left, out_from_right = shift(back_right, 1), shift(out_left, -1)
    (out_sum,) = call(add_kernel, (out_via, out_right), (table,), slots * width)
    (back_sum,) = call(add_kernel, (back_via, back_left), (longer,), slots * width)
    out_from_left, back_from_right = shift(out_sum, 1), shift(back_sum, -1)
    (joined,) = call(
        join_kernel,
        (out_own, out_from_left, out_from_right, back_own, back_from_left, back_from_right),
        (jax.ShapeDtypeStruct((slots, 2 * width + 128), BF),),
        2 * slots * slots * 128,
    )
    back = exchange(joined)
    return call(
        functools.partial(mix_kernel, cap),
        (ids, probs, back.reshape(slots, -1)),
        (
            jax.ShapeDtypeStruct(tokens.shape, BF),
            jax.ShapeDtypeStruct(tokens.shape, BF),
            jax.ShapeDtypeStruct(gate_probs.shape, F32),
        ),
        2 * slots * width * 32,
    )


def solution(mesh):
    placed = (
        P("expert", "tensor"),
        P("expert", "tensor"),
        P("expert", None),
        P("expert", None),
        P("expert", None, "tensor"),
        P("expert", None, "tensor"),
        P("expert", "tensor", None),
    )
    return jax.shard_map(
        per_device,
        mesh=mesh,
        in_specs=placed,
        out_specs=(P("expert", "tensor"), P("expert", "tensor"), P("expert", None)),
        check_vma=False,
    )
```
